32 devices in a mesh: row: 4 (over z), col: 8 (over y, x, core).
Axes of the slice: x: 2, y: 2, z: 4, core: 2. Of those that a mesh axis runs over, the one named last changes fastest.
Arguments:
- latent: bfloat16 [4, 64, 128, 16], P(None, 'row', 'col')
- conv_weight: bfloat16 [432, 2560], replicated, may hold values from -0.3125 to 0.3125
- conv_bias: float32 [2560], replicated, may hold values from -3 to 3
- norm_gain: float32 [2560], replicated, may hold values from 0.1 to 1.9
- norm_bias: float32 [2560], replicated, may hold values from -3 to 3
- qkv_weight: bfloat16 [2560, 3840], replicated
- shifts: int32 [3], replicated, may hold values from 0 to 7, as said below
Outputs:
- attended: bfloat16 [4, 64, 128, 1280], P(None, 'row', 'col')
The draws below stay inside these ranges and needn't reach their ends.
Inputs may be any that keep to these rules, and one draw needn't show every extreme that they name: shifts[0] is below 2, shifts[1] below 8, shifts[2] below 8.
All inputs are finite; a program needn't handle non-finite values.
Results may differ from the reference program's by a relative error of at most 0.007.
The reference program's roundings to bfloat16 on the way count: a program that leaves them out, or rounds other values in their place, can miss the bound.
Values may be sent and summed in bfloat16 or wider, within the bound.
A program may use at most 192 MiB of HBM per device.

```python
import jax
import jax.numpy as jnp
from jax import lax

CL = 16
GROUPS = 32
D = 2560
HEADS = 10
HD = 128
WT = 2
WH = 8
WW = 8
FR = 4
NH = 64
NW = 128


def draw_latent(key, part):
    rows = jnp.arange(NH, dtype=jnp.float32) / NH
    cols = jnp.arange(NW, dtype=jnp.float32) / NW
    ramp = 1.0 + rows[:, None] + cols[None, :]
    base = jnp.clip(jax.random.normal(key, (FR, NH, NW, CL), jnp.float32), -4.0, 4.0)
    return (base * ramp[None, :, :, None]).astype(jnp.bfloat16)


def draw_qkv_weight(key, part):
    width = 3 * HEADS * HD
    base = jnp.clip(jax.random.normal(key, (D, width), jnp.float32), -4.0, 4.0)
    return (base / D ** 0.5).astype(jnp.bfloat16)


def draw_shifts(key, part):
    first = jax.random.randint(jax.random.fold_in(key, 11), (), 0, WT)
    other = jax.random.randint(jax.random.fold_in(key, 12), (), 0, WH)
    picker = jax.random.randint(jax.random.fold_in(key, 13), (), 0, 2)
    second = jnp.where(picker == 0, WH - 1, other)
    third = jnp.where(picker == 0, other, WW - 1)
    return jnp.stack([first, second, third]).astype(jnp.int32)


def normal_values(key, shape, deviation, most, kind=jnp.bfloat16):
    return jnp.clip(deviation * jax.random.normal(key, shape, jnp.float32), -most, most).astype(kind)


def setup_inputs(seed: int = 0) -> dict:
    key_of = jax.random.split(jax.random.key(seed), 8)
    return {
        "latent": draw_latent(jax.random.fold_in(key_of[7], 71), 0),
        "conv_weight": normal_values(key_of[1], (27 * CL, D), (27 * CL) ** -0.5, 0.3125),
        "conv_bias": normal_values(key_of[2], (D,), 0.5, 3.0, jnp.float32),
        "norm_gain": jnp.clip(1.0 + 0.18 * jax.random.normal(key_of[3], (D,), jnp.float32), 0.1, 1.9),
        "norm_bias": normal_values(key_of[4], (D,), 0.5, 3.0, jnp.float32),
        "qkv_weight": draw_qkv_weight(jax.random.fold_in(key_of[7], 71), 0),
        "shifts": draw_shifts(jax.random.fold_in(key_of[7], 71), 0),
    }


def conv_taps(padded, frames, rows, cols):
    padded = jnp.concatenate([padded[:1], padded[:1], padded], 0)
    taps = [padded[a:a + frames, b:b + rows, c:c + cols] for a in range(3) for b in range(3) for c in range(3)]
    return jnp.concatenate(taps, -1).reshape(frames * rows * cols, -1)

def window_attend(block):
    frames, rows, cols = (block.shape[0], block.shape[1], block.shape[2])
    nt, na, nb = (frames // WT, rows // WH, cols // WW)
    grid = block.reshape(nt, WT, na, WH, nb, WW, 3, HEADS, HD)
    grid = grid.transpose(0, 2, 4, 6, 7, 1, 3, 5, 8).reshape(nt, na, nb, 3, HEADS, WT * WH * WW, HD)
    query = grid[:, :, :, 0].astype(jnp.float32)
    keys = grid[:, :, :, 1].astype(jnp.float32)
    values = grid[:, :, :, 2].astype(jnp.float32)
    scores = jnp.einsum('tabhqd,tabhkd->tabhqk', query, keys) * (1.0 / HD ** 0.5)
    probs = jax.nn.softmax(scores, axis=-1).astype(jnp.bfloat16)
    result = jnp.einsum('tabhqk,tabhkd->tabhqd', probs.astype(jnp.float32), values).astype(jnp.bfloat16)
    result = result.reshape(nt, na, nb, HEADS, WT, WH, WW, HD).transpose(0, 4, 1, 5, 2, 6, 3, 7)
    return result.reshape(frames, rows, cols, HEADS * HD)

def reference(latent, conv_weight, conv_bias, norm_gain, norm_bias, qkv_weight, shifts):
    frames, rows, cols = (latent.shape[0], latent.shape[1], latent.shape[2])
    padded = jnp.pad(latent, ((0, 0), (1, 1), (1, 1), (0, 0)))
    stacked = conv_taps(padded, frames, rows, cols)
    hidden = jnp.dot(stacked, conv_weight, preferred_element_type=jnp.float32) + conv_bias
    grouped = hidden.reshape(-1, GROUPS, D // GROUPS)
    mean = lax.optimization_barrier(jnp.mean(grouped, axis=(0, 2)))
    centred = grouped - mean[None, :, None]
    var = lax.optimization_barrier(jnp.mean(centred * centred, axis=(0, 2)))
    normed = (centred / jnp.sqrt(var + 1e-05)[None, :, None]).reshape(-1, D) * norm_gain + norm_bias
    feat = jax.nn.silu(normed).astype(jnp.bfloat16)
    packed = jnp.dot(feat, qkv_weight, preferred_element_type=jnp.float32).astype(jnp.bfloat16)
    packed = packed.reshape(frames, rows, cols, 3 * HEADS * HD)
    rolled = jnp.roll(packed, -shifts[0], axis=0)
    rolled = jnp.roll(rolled, -shifts[1], axis=1)
    rolled = jnp.roll(rolled, -shifts[2], axis=2)
    blocks = rolled.reshape(frames // WT, WT, rows, cols, 3 * HEADS * HD)
    result = lax.map(window_attend, blocks).reshape(frames, rows, cols, HEADS * HD)
    result = jnp.roll(result, shifts[0], axis=0)
    result = jnp.roll(result, shifts[1], axis=1)
    return jnp.roll(result, shifts[2], axis=2)
```

```python
import functools
import math

import jax
import jax.numpy as jnp
from jax import lax
from jax.experimental import pallas as pl
from jax.experimental.pallas import tpu as pltpu
from jax.sharding import PartitionSpec as P

CL = 16
GROUPS = 32
D = 2560
HEADS = 10
HD = 128
WT = 2
WH = 8
WW = 8
HALF = 4


def shifted(x, axis, by):
    length = lax.axis_size(axis)
    return lax.ppermute(x, axis, [(i, (i + by) % length) for i in range(length)])


def signed_shift(shift, window):
    return jnp.where(shift <= HALF, shift, shift - window)


CELLS = WT * WH * WW
PAIR = 2 * HD


def attend_kernel(
    dims, stacked, conv_weight, slope, offset, wq, wk, wv, moves, out, feat, qkv
):
    frames, rows, cols = dims
    total = frames * rows * cols

    @pl.when(pl.program_id(0) == 0)
    def _():
        part = 256

        @pl.loop(0, total // part)
        def _(i):
            start = pl.multiple_of(i * part, part)
            block = stacked[pl.ds(start, part), :]
            for n in range(0, D, 512):
                hidden = jnp.dot(
                    block, conv_weight[:, n : n + 512], preferred_element_type=jnp.float32
                )
                half = hidden * slope[:, n : n + 512] + offset[:, n : n + 512]
                feat[pl.ds(start, part), n : n + 512] = (half + half * jnp.tanh(half)).astype(
                    jnp.bfloat16
                )

    def project(start, j):
        if start < total:
            lines = slice(start, start + CHUNK)
            qkv[lines, j * PAIR : (j + 1) * PAIR] = jnp.dot(
                feat[lines, :], (wq, wk, wv)[j][...], preferred_element_type=jnp.float32
            ).astype(jnp.bfloat16)

    def part(item, j):
        window, head = item
        first = j * PAIR + head * HD
        return qkv[window * CELLS : (window + 1) * CELLS, first : first + HD]

    def score(item):
        return lax.dot_general(
            part(item, 0), part(item, 1), (((1,), (1,)), ((), ())), preferred_element_type=jnp.float32
        )

    def softmax(scores):
        most = [jnp.max(x, axis=-1, keepdims=True) for x in scores]
        powers = [
            jnp.exp2((x - m) * (math.log2(math.e) / HD**0.5)) for x, m in zip(scores, most)
        ]
        sums = [jnp.sum(x, axis=-1, keepdims=True) for x in powers]
        return [(x * (1.0 / t)).astype(jnp.bfloat16) for x, t in zip(powers, sums)]

    across = cols // WW

    def store(group, head, results):
        t, a = group // (rows // WH), group % (rows // WH)
        merged = jnp.concatenate([x.reshape(WT, WH, WW, HD) for x in results], 2)
        for dt in range(WT):
            frame = lax.rem(t * WT + dt + moves[0], frames)
            for y in range(WH):
                row = lax.rem(a * WH + y + moves[1], rows)
                line = pltpu.roll(merged[dt, y], moves[2], 0).astype(jnp.bfloat16)
                out[frame, row, :, head * HD : (head + 1) * HD] = line

    for j in range(3):
        project(0, j)
    for start in range(0, total, CHUNK):
        first = start // CELLS
        items = [(w, head) for head in range(2) for w in range(first, first + CHUNK // CELLS)]
        scores = [score(item) for item in items]
        project(start + CHUNK, 0)
        probs = softmax(scores)
        project(start + CHUNK, 1)
        results = {
            item: jnp.dot(p, part(item, 2), preferred_element_type=jnp.float32)
            for item, p in zip(items, probs)
        }
        project(start + CHUNK, 2)
        for head in range(2):
            for w in range(first, first + CHUNK // CELLS, across):
                store(w // across, head, [results[w + b, head] for b in range(across)])


CHUNK = 512


def attend(dims, stacked, conv_weight, slope, offset, qkv_weight, moves):
    frames, rows, cols = dims
    total = frames * rows * cols
    steps = HEADS // 2

    def whole(x):
        return pl.BlockSpec(x.shape, lambda h: (0,) * x.ndim, pipeline_mode=pl.Buffered(1))

    def columns(j):
        return pl.BlockSpec((D, PAIR), lambda h: (0, j * steps + h))

    return pl.pallas_call(
        functools.partial(attend_kernel, dims),
        grid=(steps,),
        out_shape=jax.ShapeDtypeStruct((frames, rows, cols, HEADS * HD), jnp.bfloat16),
        in_specs=[
            whole(stacked),
            whole(conv_weight),
            whole(slope),
            whole(offset),
            columns(0),
            columns(1),
            columns(2),
            pl.BlockSpec(memory_space=pltpu.SMEM),
        ],
        out_specs=pl.BlockSpec((frames, rows, cols, PAIR), lambda h: (0, 0, 0, h)),
        scratch_shapes=[
            pltpu.VMEM((total, D), jnp.bfloat16),
            pltpu.VMEM((total, 3 * PAIR), jnp.bfloat16),
        ],
        compiler_params=pltpu.CompilerParams(vmem_limit_bytes=48 * 1024 * 1024),
    )(stacked, conv_weight, slope, offset, qkv_weight, qkv_weight, qkv_weight, moves)


MESH = pl.DeviceIdType.MESH
LANES = 128
TAPS = 9
DEEP = 4 * LANES
SPAN = 640
EPS = 1e-05


def tap_rows():
    moves = []
    for a in range(3):
        for c in range(3):
            for b in range(3):
                place = c * 3 + b
                target = a * LANES + place * CL if place < 8 else 3 * LANES + a * CL
                moves.append((((a * 3 + b) * 3 + c) * CL, target))
    return moves


def front_kernel(
    dims,
    latent,
    conv_weight,
    bias,
    gain,
    beta,
    shifts,
    stacked,
    packed_out,
    slope,
    offset,
    field,
    moved,
    wide,
    thin,
    packed,
    sums,
    squares,
    means,
    scales,
    part,
    arrived,
    weight_sems,
    halo_send,
    halo_recv,
    sum_send,
    sum_recv,
    out_sem,
):
    frames, rows, cols = dims
    n_row, n_col = lax.axis_size("row"), lax.axis_size("col")
    me_row, me_col = lax.axis_index("row"), lax.axis_index("col")
    down, up = lax.rem(me_row + 1, n_row), lax.rem(me_row + n_row - 1, n_row)
    right, left = lax.rem(me_col + 1, n_col), lax.rem(me_col + n_col - 1, n_col)

    groups = []
    for axis, me, count in (("col", me_col, n_col), ("row", me_row, n_row)):
        groups.append([{axis: lax.rem(me + k, count)} for k in range(1, count)])
    corners = [{"row": r, "col": c} for r in (down, up) for c in (right, left)]
    peers = groups[0] + groups[1] + corners
    barrier = pltpu.get_barrier_semaphore()
    for peer in peers:
        pl.semaphore_signal(barrier, inc=1, device_id=peer, device_id_type=MESH)

    loads = []
    for k, (source, target) in enumerate(tap_rows()):
        loads.append(
            pltpu.make_async_copy(
                conv_weight.at[pl.ds(source, CL)], packed.at[pl.ds(target, CL)], weight_sems.at[k]
            )
        )
        loads[-1].start()
    filled = 3 * LANES + 3 * CL
    packed[filled:, :] = jnp.zeros((DEEP - filled, D), jnp.bfloat16)

    lane16 = lax.broadcasted_iota(jnp.int32, (CL, LANES), 1)
    chan = lax.broadcasted_iota(jnp.int32, (CL, LANES), 0)
    for half in range(2):
        total = jnp.zeros((frames * cols, LANES), jnp.float32)
        for y in range(8):
            pick = jnp.where(lane16 == chan + y * CL, 1.0, 0.0).astype(jnp.bfloat16)
            line = latent[:, half * 8 + y].reshape(frames * cols, CL)
            total = total + jnp.dot(line, pick, preferred_element_type=jnp.float32)
        lanes = slice((1 + half) * LANES, (2 + half) * LANES)
        field[:, 8:24, lanes] = total.reshape(frames, cols, LANES)

    pl.semaphore_wait(barrier, len(peers))

    first, last, both = (8, 8), (16, 8), (8, 16)
    x_low, x_high = (0, 8), (24, 8)
    y_first, y_last, y_both = (LANES, LANES), (2 * LANES, LANES), (LANES, 2 * LANES)
    y_low, y_high = (0, LANES), (3 * LANES, LANES)
    plan = [
        ({"col": right}, last, y_both, x_low, y_both),
        ({"col": left}, first, y_both, x_high, y_both),
        ({"row": down}, both, y_last, both, y_low),
        ({"row": up}, both, y_first, both, y_high),
        (corners[0], last, y_last, x_low, y_low),
        (corners[1], first, y_last, x_high, y_low),
        (corners[2], last, y_first, x_low, y_high),
        (corners[3], first, y_first, x_high, y_high),
    ]
    halos = []
    for k, (peer, sx, sy, dx, dy) in enumerate(plan):
        halos.append(
            pltpu.make_async_remote_copy(
                src_ref=field.at[:, pl.ds(*sx), pl.ds(*sy)],
                dst_ref=field.at[:, pl.ds(*dx), pl.ds(*dy)],
                send_sem=halo_send.at[k],
                recv_sem=halo_recv.at[k],
                device_id=peer,
                device_id_type=MESH,
            )
        )
        halos[-1].start()

    move_row = signed_shift(shifts[1], WH)
    move_col = signed_shift(shifts[2], WW)
    for copy in halos:
        copy.wait()

    lines = pltpu.roll(field[...].reshape(frames * 32, DEEP), 400 - 16 * move_row, 1)
    lines = lines[:, : 3 * LANES].reshape(frames, 32, 3 * LANES)
    moved[...] = pltpu.roll(lines, 25 - move_col, 1)

    lane = lax.broadcasted_iota(jnp.int32, (frames * cols, LANES), 1)
    place = lax.broadcasted_iota(jnp.int32, (frames * cols, LANES), 0) % cols
    wide_cols, wide_rows = n_col * cols, n_row * rows
    at_col = lax.rem(me_col * cols + move_col + place + wide_cols, wide_cols)
    pieces = []
    for c in range(3):
        piece = moved[:, c : c + cols, :].reshape(frames * cols, 3 * LANES)
        parts = [piece[:, k * LANES : (k + 1) * LANES] for k in range(3)]
        if c == 0:
            parts = [jnp.where(at_col == 0, 0.0, p) for p in parts]
        if c == 2:
            parts = [jnp.where(at_col == wide_cols - 1, 0.0, p) for p in parts]
        pieces.append(parts)
    row_tap = (lane // CL) % 3

    def line_of(y):
        at_row = lax.rem(me_row * rows + move_row + y + wide_rows, wide_rows)
        turned = []
        for c in range(3):
            k, start = divmod(y * CL, LANES)
            value = pieces[c][k]
            if start + 48 > LANES:
                value = jnp.where(lane < start + 48 - LANES, pieces[c][k + 1], value)
            turned.append(pltpu.roll(value, (c * 48 - start) % LANES, 1))
        full = jnp.where(lane < 48, turned[0], jnp.where(lane < 96, turned[1], turned[2]))
        gone = jnp.where(at_row == 0, 0, -1)
        full = jnp.where(row_tap == gone, 0.0, full)
        gone = jnp.where(at_row == wide_rows - 1, 2, -1)
        full = jnp.where(row_tap == gone, 0.0, full)
        some = jnp.where(lane < jnp.where(at_row == wide_rows - 1, 0, CL), turned[2], 0.0)
        return full, some

    for y in range(0, rows, 2):
        fulls, somes = zip(*[line_of(y + k) for k in range(2)])
        a, h = divmod(y, WH)
        full = jnp.concatenate([v.reshape(frames, cols // WW, WW, LANES) for v in fulls], 2)
        some = jnp.concatenate([v.reshape(frames, cols // WW, WW, LANES) for v in somes], 2)
        for b in range(cols // WW):
            lines16 = slice(((a * (cols // WW)) + b) * 64 + h * WW, ((a * (cols // WW)) + b) * 64 + h * WW + 16)
            wide[:, lines16, :] = full[:, b].astype(jnp.bfloat16)
            thin[:, lines16, :] = some[:, b]

    for t in range(frames):
        frame = lax.rem(shifts[0] + t, frames)
        sources = [jnp.maximum(frame - 2, 0), jnp.maximum(frame - 1, 0), frame]
        rest = thin[sources[0]]
        rest = rest + pltpu.roll(thin[sources[1]], CL, 1)
        rest = rest + pltpu.roll(thin[sources[2]], 2 * CL, 1)
        blocks = [wide[f] for f in sources] + [rest.astype(jnp.bfloat16)]
        for w in range(rows * cols // 64):
            start = ((t // WT) * (rows * cols // 64) + w) * CELLS + (t % WT) * 64
            for k in range(4):
                stacked[start : start + 64, k * LANES : (k + 1) * LANES] = blocks[k][w * 64 : w * 64 + 64]

    for copy in loads:
        copy.wait()
    keep = pltpu.make_async_copy(packed, packed_out, out_sem)
    keep.start()

    total = frames * rows * cols
    sums[...] = jnp.zeros_like(sums)
    squares[...] = jnp.zeros_like(squares)

    @pl.loop(0, total // 256)
    def _(i):
        block = stacked[pl.ds(pl.multiple_of(i * 256, 256), 256), :]
        for n in range(0, D, 512):
            hidden = jnp.dot(block, packed[:, n : n + 512], preferred_element_type=jnp.float32)
            grouped = hidden.reshape(32, 8, 512)
            sums[:, n : n + 512] += jnp.sum(grouped, axis=0)
            squares[:, n : n + 512] += jnp.sum(grouped * grouped, axis=0)

    first_sums, second_sums = sums[...], squares[...]
    for by in (4, 2, 1):
        first_sums = first_sums + pltpu.roll(first_sums, by, 0)
        second_sums = second_sums + pltpu.roll(second_sums, by, 0)
    second_sums = second_sums + bias[...] * (2.0 * first_sums + total * bias[...])
    first_sums = first_sums + total * bias[...]

    sub = lax.broadcasted_iota(jnp.int32, (8, LANES), 0)
    lane8 = lax.broadcasted_iota(jnp.int32, (8, LANES), 1)
    width = D // GROUPS
    segments = []
    for i in range(SPAN // LANES):
        value = jnp.zeros((8, LANES), jnp.float32)
        for s in range(D // SPAN):
            lanes = slice(s * SPAN + i * LANES, s * SPAN + (i + 1) * LANES)
            value = jnp.where(sub == s, first_sums[:, lanes], value)
            value = jnp.where(sub == s + 4, second_sums[:, lanes], value)
        segments.append(value)
    table = jnp.zeros((8, LANES), jnp.float32)
    for j in range(SPAN // width):
        low, high = j * width, (j + 1) * width
        column = jnp.zeros((8, LANES), jnp.float32)
        for i in range(SPAN // LANES):
            start = i * LANES
            if low < start + LANES and high > start:
                inside = (lane8 >= low - start) & (lane8 < high - start)
                column = column + jnp.where(inside, segments[i], 0.0)
        table = jnp.where(lane8 == j, jnp.sum(column, axis=1, keepdims=True), table)

    part[0] = table
    slot = 0
    for phase, group in enumerate(groups):
        copies = []
        for k, peer in enumerate(group):
            copies.append(
                pltpu.make_async_remote_copy(
                    src_ref=part.at[phase],
                    dst_ref=arrived.at[slot + k],
                    send_sem=sum_send.at[slot + k],
                    recv_sem=sum_recv.at[slot + k],
                    device_id=peer,
                    device_id_type=MESH,
                )
            )
            copies[-1].start()
        table = part[phase]
        for k, copy in enumerate(copies):
            copy.wait()
            table = table + arrived[slot + k]
        part[phase + 1] = table
        slot += len(group)

    count = total * n_row * n_col * width
    mean = table * (1.0 / count)
    var = pltpu.roll(mean, 4, 0) - mean * mean
    scale = lax.rsqrt(var + EPS)
    for i in range(SPAN // LANES):
        mean_here = jnp.zeros((8, LANES), jnp.float32)
        scale_here = jnp.zeros((8, LANES), jnp.float32)
        for j in range(SPAN // width):
            low, high = j * width - i * LANES, (j + 1) * width - i * LANES
            if low < LANES and high > 0:
                inside = (lane8 >= low) & (lane8 < high)
                mean_here = jnp.where(inside, mean[:, j : j + 1], mean_here)
                scale_here = jnp.where(inside, scale[:, j : j + 1], scale_here)
        for s in range(D // SPAN):
            lanes = slice(s * SPAN + i * LANES, s * SPAN + (i + 1) * LANES)
            means[:, lanes] = mean_here[s : s + 1]
            scales[:, lanes] = scale_here[s : s + 1]
    steep = 0.5 * scales[...] * gain[...]
    slope[...] = steep
    offset[...] = (bias[...] - means[...]) * steep + 0.5 * beta[...]
    keep.wait()


def front(dims, latent, conv_weight, conv_bias, norm_gain, norm_bias, shifts):
    frames, rows, cols = dims
    total = frames * rows * cols
    count = lax.axis_size("row") + lax.axis_size("col") - 2
    vmem = pl.BlockSpec(memory_space=pltpu.VMEM)
    hbm = pl.BlockSpec(memory_space=pl.ANY)
    return pl.pallas_call(
        functools.partial(front_kernel, dims),
        out_shape=[
            jax.ShapeDtypeStruct((total, DEEP), jnp.bfloat16),
            jax.ShapeDtypeStruct((DEEP, D), jnp.bfloat16),
            jax.ShapeDtypeStruct((1, D), jnp.float32),
            jax.ShapeDtypeStruct((1, D), jnp.float32),
        ],
        in_specs=[vmem, hbm, vmem, vmem, vmem, pl.BlockSpec(memory_space=pltpu.SMEM)],
        out_specs=[vmem, hbm, vmem, vmem],
        scratch_shapes=[
            pltpu.VMEM((frames, 32, DEEP), jnp.float32),
            pltpu.VMEM((frames, 32, 3 * LANES), jnp.float32),
            pltpu.VMEM((frames, rows * cols, LANES), jnp.bfloat16),
            pltpu.VMEM((frames, rows * cols, LANES), jnp.float32),
            pltpu.VMEM((DEEP, D), jnp.bfloat16),
            pltpu.VMEM((8, D), jnp.float32),
            pltpu.VMEM((8, D), jnp.float32),
            pltpu.VMEM((1, D), jnp.float32),
            pltpu.VMEM((1, D), jnp.float32),
            pltpu.VMEM((3, 8, LANES), jnp.float32),
            pltpu.VMEM((count, 8, LANES), jnp.float32),
            pltpu.SemaphoreType.DMA((27,)),
            pltpu.SemaphoreType.DMA((8,)),
            pltpu.SemaphoreType.DMA((8,)),
            pltpu.SemaphoreType.DMA((count,)),
            pltpu.SemaphoreType.DMA((count,)),
            pltpu.SemaphoreType.DMA,
        ],
        compiler_params=pltpu.CompilerParams(
            collective_id=1, has_side_effects=True, vmem_limit_bytes=32 * 1024 * 1024
        ),
    )(latent, conv_weight, conv_bias[None], norm_gain[None], norm_bias[None], shifts)


def send_back(result, axis, dim, move, window, least_sent):
    size = result.shape[dim]

    def branch(by):
        def run(field):
            if by == 0:
                return field
            count = abs(by)
            wide = max(count, least_sent)
            start = 0 if by > 0 else size - wide
            part = lax.slice_in_dim(field, start, start + wide, axis=dim)
            shape = part.shape
            part = lax.optimization_barrier(part.reshape(-1, shape[-1]))
            arrived = lax.optimization_barrier(shifted(part, axis, 1 if by > 0 else -1))
            skip = 0 if by > 0 else wide - count
            arrived = lax.slice_in_dim(arrived.reshape(shape), skip, skip + count, axis=dim)
            return lax.dynamic_update_slice_in_dim(field, arrived, start + skip, dim)

        return run

    least = HALF + 1 - window
    return lax.switch(move - least, [branch(by) for by in range(least, HALF + 1)], result)


def per_device(latent, conv_weight, conv_bias, norm_gain, norm_bias, qkv_weight, shifts):
    dims = (latent.shape[0], latent.shape[1], latent.shape[2])
    frames, rows, cols = dims
    stacked, packed, slope, offset = front(
        dims, latent, conv_weight, conv_bias, norm_gain, norm_bias, shifts
    )
    move_row = signed_shift(shifts[1], WH)
    move_col = signed_shift(shifts[2], WW)
    moves = jnp.stack([shifts[0], (move_row + rows) % rows, (move_col + cols) % cols])
    result = attend(dims, stacked, packed, slope, offset, qkv_weight, moves)
    result = send_back(result, "row", 1, move_row, WH, 1)
    return send_back(result, "col", 2, move_col, WW, 2)


def solution(mesh):
    in_specs = (P(None, "row", "col", None), P(), P(), P(), P(), P(), P())
    out_specs = P(None, "row", "col", None)
    return jax.shard_map(
        per_device, mesh=mesh, in_specs=in_specs, out_specs=out_specs, check_vma=False
    )
```

```python
import functools
import math

import jax
import jax.numpy as jnp
from jax import lax
from jax.experimental import pallas as pl
from jax.experimental.pallas import tpu as pltpu
from jax.sharding import PartitionSpec as P

CL = 16
GROUPS = 32
D = 2560
HEADS = 10
HD = 128
WT = 2
WH = 8
WW = 8
HALF = 4


def signed_shift(shift, window):
    return jnp.where(shift <= HALF, shift, shift - window)


CELLS = WT * WH * WW
PAIR = 2 * HD


STEPS = HEADS // 2


def attend_kernel(
    dims,
    way,
    stacked,
    conv_weight,
    slope,
    offset,
    wq,
    wk,
    wv,
    own_out,
    row_out,
    col_out,
    corner_out,
    feat,
    qkv,
    own,
    edge,
    own_sems,
    row_send,
    row_recv,
    col_send,
    col_recv,
    corner_send,
    corner_recv,
):
    frames, rows, cols = dims
    total = frames * rows * cols
    step = pl.program_id(0)
    n_row, n_col = lax.axis_size("row"), lax.axis_size("col")
    me_row, me_col = lax.axis_index("row"), lax.axis_index("col")
    negative_row, negative_col = way // 2, way % 2
    to_row = {"row": lax.rem(me_row + (n_row - 1 if negative_row else 1), n_row)}
    from_row = {"row": lax.rem(me_row + (1 if negative_row else n_row - 1), n_row)}
    to_col = {"col": lax.rem(me_col + (n_col - 1 if negative_col else 1), n_col)}
    from_col = {"col": lax.rem(me_col + (1 if negative_col else n_col - 1), n_col)}
    across, deep = cols // WW, frames // WT
    row_edge = 0 if negative_row else rows // WH - 1
    col_edge = 0 if negative_col else across - 1
    order = [row_edge] + [a for a in range(rows // WH) if a != row_edge]

    def sends(p, a):
        copies = [
            pltpu.make_async_remote_copy(
                src_ref=edge.at[p, a],
                dst_ref=col_out.at[p, a],
                send_sem=col_send.at[p, a],
                recv_sem=col_recv.at[p, a],
                device_id=to_col,
                device_id_type=MESH,
            )
        ]
        if a == row_edge:
            lines = pl.ds(0 if negative_row else 32, 32)
            copies.append(
                pltpu.make_async_remote_copy(
                    src_ref=own.at[p, pl.ds(a * across, across), :, lines],
                    dst_ref=row_out.at[p],
                    send_sem=row_send.at[p],
                    recv_sem=row_recv.at[p],
                    device_id=to_row,
                    device_id_type=MESH,
                )
            )
            lines = pl.ds(0 if negative_row else 16, 16)
            copies.append(
                pltpu.make_async_remote_copy(
                    src_ref=edge.at[p, a, :, lines],
                    dst_ref=corner_out.at[p],
                    send_sem=corner_send.at[p],
                    recv_sem=corner_recv.at[p],
                    device_id=to_row | to_col,
                    device_id_type=MESH,
                )
            )
        return copies

    def keeps(p):
        return pltpu.make_async_copy(own.at[p], own_out.at[p], own_sems.at[p])

    def project(into, j):
        qkv[into, :, j * PAIR : (j + 1) * PAIR] = jnp.dot(
            feat[...], (wq, wk, wv)[j][...], preferred_element_type=jnp.float32
        ).astype(jnp.bfloat16)

    sub = lax.broadcasted_iota(jnp.int32, (8, 8, HD), 1)
    sub = sub[: 4]

    def attention(p, source):
        def part(item, j):
            window, head = item
            first = j * PAIR + head * HD
            return qkv[source, window * CELLS : (window + 1) * CELLS, first : first + HD]

        def score(item):
            return lax.dot_general(
                part(item, 0), part(item, 1), (((1,), (1,)), ((), ())), preferred_element_type=jnp.float32
            )

        def softmax(scores):
            most = [jnp.max(x, axis=-1, keepdims=True) for x in scores]
            powers = [
                jnp.exp2((x - m) * (math.log2(math.e) / HD**0.5)) for x, m in zip(scores, most)
            ]
            sums = [jnp.sum(x, axis=-1, keepdims=True) for x in powers]
            return [(x * (1.0 / t)).astype(jnp.bfloat16) for x, t in zip(powers, sums)]

        def items(a):
            return [(w, head) for head in range(2) for w in range(a * deep * across, (a + 1) * deep * across)]

        def store(a, item, result):
            window, head = item
            t2, b = divmod(window - a * deep * across, across)
            lanes = slice(head * HD, (head + 1) * HD)
            halves = result.reshape(WT, WH * WW, HD)
            for t in range(WT):
                own[p, a * across + b, t2 * WT + t, :, lanes] = halves[t].astype(jnp.bfloat16)
            if b == col_edge:
                lines = result.reshape(WT, WH // 2, 2, WW, HD)
                for t in range(WT):
                    even, odd = lines[t, :, 0], lines[t, :, 1]
                    if negative_col:
                        packed = jnp.where(sub < 4, even, pltpu.roll(odd, 4, 1))
                    else:
                        packed = jnp.where(sub < 4, pltpu.roll(even, 4, 1), odd)
                    edge[p, a, t2 * WT + t, :, lanes] = packed.reshape(WH * HALF, HD).astype(jnp.bfloat16)

        def apply(names, probs):
            return [
                jnp.dot(x, part(item, 2), preferred_element_type=jnp.float32)
                for item, x in zip(names, probs)
            ]

        return items, score, softmax, apply, store

    def run(p, source, into):
        items, score, softmax, apply, store = attention(p, source)
        waiting = [score(item) for item in items(order[0])]
        for k, a in enumerate(order):
            if into is not None:
                project(into, k)
            probs = softmax(waiting)
            results = apply(items(a), probs)
            if k + 1 < len(order):
                waiting = [score(item) for item in items(order[k + 1])]
            for item, result in zip(items(a), results):
                store(a, item, result)
            for copy in sends(p, a):
                copy.start()
        if into is not None:
            project(into, 2)
        keeps(p).start()

    @pl.when(step == 0)
    def _():
        barrier = pltpu.get_barrier_semaphore()
        for peer in (from_row, from_col, from_row | from_col):
            pl.semaphore_signal(barrier, inc=1, device_id=peer, device_id_type=MESH)
        part = 256

        @pl.loop(0, total // part)
        def _(i):
            start = pl.multiple_of(i * part, part)
            block = stacked[pl.ds(start, part), :]
            for n in range(0, D, 512):
                hidden = jnp.dot(
                    block, conv_weight[:, n : n + 512], preferred_element_type=jnp.float32
                )
                half = hidden * slope[:, n : n + 512] + offset[:, n : n + 512]
                feat[pl.ds(start, part), n : n + 512] = (half + half * jnp.tanh(half)).astype(
                    jnp.bfloat16
                )

        for j in range(3):
            project(0, j)
        pl.semaphore_wait(barrier, 3)

    @pl.when((step > 0) & (step < STEPS))
    def _():
        run(step - 1, lax.rem(step - 1, 2), lax.rem(step, 2))

    @pl.when(step == STEPS)
    def _():
        run(STEPS - 1, (STEPS - 1) % 2, None)

        @pl.loop(0, STEPS)
        def _(p):
            for a in order:
                for copy in sends(p, a):
                    copy.wait()
            keeps(p).wait()


def attend(dims, way, stacked, conv_weight, slope, offset, qkv_weight):
    frames, rows, cols = dims
    total = frames * rows * cols
    quarters = (rows // WH) * (cols // WW)

    def whole(x):
        return pl.BlockSpec(x.shape, lambda h: (0,) * x.ndim, pipeline_mode=pl.Buffered(1))

    def columns(j):
        return pl.BlockSpec((D, PAIR), lambda h: (0, j * STEPS + jnp.minimum(h, STEPS - 1)))

    hbm = pl.BlockSpec(memory_space=pl.ANY)
    own = (STEPS, quarters, frames, WH * WW, PAIR)
    row = (STEPS, cols // WW, frames, HALF * WW, PAIR)
    col = (STEPS, rows // WH, frames, HALF * WH, PAIR)
    corner = (STEPS, frames, HALF * HALF, PAIR)
    dma = pltpu.SemaphoreType.DMA
    return pl.pallas_call(
        functools.partial(attend_kernel, dims, way),
        grid=(STEPS + 1,),
        out_shape=[jax.ShapeDtypeStruct(shape, jnp.bfloat16) for shape in (own, row, col, corner)],
        in_specs=[
            whole(stacked),
            whole(conv_weight),
            whole(slope),
            whole(offset),
            columns(0),
            columns(1),
            columns(2),
        ],
        out_specs=[hbm] * 4,
        scratch_shapes=[
            pltpu.VMEM((total, D), jnp.bfloat16),
            pltpu.VMEM((2, total, 3 * PAIR), jnp.bfloat16),
            pltpu.VMEM(own, jnp.bfloat16),
            pltpu.VMEM(col, jnp.bfloat16),
            dma((STEPS,)),
            dma((STEPS,)),
            dma((STEPS,)),
            dma((STEPS, rows // WH)),
            dma((STEPS, rows // WH)),
            dma((STEPS,)),
            dma((STEPS,)),
        ],
        compiler_params=pltpu.CompilerParams(
            collective_id=2 + way, has_side_effects=True, vmem_limit_bytes=48 * 1024 * 1024
        ),
    )(stacked, conv_weight, slope, offset, qkv_weight, qkv_weight, qkv_weight)


def place_kernel(dims, shifts, own, row, col, corner, out, field):
    frames, rows, cols = dims
    across = cols // WW
    move_row = signed_shift(shifts[1], WH)
    move_col = signed_shift(shifts[2], WW)
    high, long = rows + HALF, cols + WW
    turn = lax.rem(move_col + long, long)

    def spread(value):
        lines = value.astype(jnp.float32).reshape(-1, 8, PAIR)
        low = lax.broadcasted_iota(jnp.int32, lines.shape, 1) < HALF
        other = pltpu.roll(lines, HALF, 1)
        pair = jnp.stack([jnp.where(low, lines, other), jnp.where(low, other, lines)], 1)
        return pair.reshape(-1, 8, PAIR)

    @pl.loop(0, STEPS)
    def _(p):
        for a in range(rows // WH):
            for b in range(across):
                value = own[p, a * across + b, 0].astype(jnp.float32)
                field[a * WH : (a + 1) * WH, b * WW : (b + 1) * WW] = value.reshape(WH, WW, PAIR)
            field[a * WH : (a + 1) * WH, cols:] = spread(col[p, a, 0])
        for b in range(across):
            value = row[p, b, 0].astype(jnp.float32)
            field[rows:, b * WW : (b + 1) * WW] = value.reshape(HALF, WW, PAIR)
        field[rows:, cols:] = spread(corner[p, 0])
        lanes = pl.ds(pl.multiple_of(p * PAIR, PAIR), PAIR)
        for y in range(rows):
            line = field[lax.rem(y - move_row + high, high)]
            out[0, y, :, lanes] = pltpu.roll(line, turn, 0)[:cols].astype(jnp.bfloat16)


def place(dims, shifts, own, row, col, corner):
    frames, rows, cols = dims

    def frame(f, shifts):
        return lax.rem(f - shifts[0] + frames, frames)

    def block(x):
        shape = x.shape[:-3] + (1,) + x.shape[-2:]
        ahead = len(shape) - 3
        return pl.BlockSpec(shape, lambda f, shifts: (0,) * ahead + (frame(f, shifts), 0, 0))

    return pl.pallas_call(
        functools.partial(place_kernel, dims),
        grid_spec=pltpu.PrefetchScalarGridSpec(
            num_scalar_prefetch=1,
            grid=(frames,),
            in_specs=[block(own), block(row), block(col), block(corner)],
            out_specs=pl.BlockSpec((1, rows, cols, HEADS * HD), lambda f, shifts: (f, 0, 0, 0)),
            scratch_shapes=[pltpu.VMEM((rows + HALF, cols + WW, PAIR), jnp.float32)],
        ),
        out_shape=jax.ShapeDtypeStruct((frames, rows, cols, HEADS * HD), jnp.bfloat16),
        compiler_params=pltpu.CompilerParams(vmem_limit_bytes=32 * 1024 * 1024),
    )(shifts, own, row, col, corner)


MESH = pl.DeviceIdType.MESH
LANES = 128
TAPS = 9
DEEP = 4 * LANES
SPAN = 640
EPS = 1e-05


def tap_rows():
    moves = []
    for a in range(3):
        for c in range(3):
            for b in range(3):
                place = c * 3 + b
                target = a * LANES + place * CL if place < 8 else 3 * LANES + a * CL
                moves.append((((a * 3 + b) * 3 + c) * CL, target))
    return moves


def front_kernel(
    dims,
    latent,
    conv_weight,
    bias,
    gain,
    beta,
    shifts,
    stacked,
    packed_out,
    slope,
    offset,
    way,
    field,
    moved,
    wide,
    thin,
    packed,
    sums,
    squares,
    means,
    scales,
    rows_of,
    part,
    arrived,
    weight_sems,
    halo_send,
    halo_recv,
    sum_send,
    sum_recv,
    out_sem,
    row_sems,
):
    frames, rows, cols = dims
    n_row, n_col = lax.axis_size("row"), lax.axis_size("col")
    me_row, me_col = lax.axis_index("row"), lax.axis_index("col")
    down, up = lax.rem(me_row + 1, n_row), lax.rem(me_row + n_row - 1, n_row)
    right, left = lax.rem(me_col + 1, n_col), lax.rem(me_col + n_col - 1, n_col)

    groups = []
    for axis, me, count in (("col", me_col, n_col), ("row", me_row, n_row)):
        groups.append([{axis: lax.rem(me + k, count)} for k in range(1, count)])
    corners = [{"row": r, "col": c} for r in (down, up) for c in (right, left)]
    peers = groups[0] + groups[1] + corners
    barrier = pltpu.get_barrier_semaphore()
    for peer in peers:
        pl.semaphore_signal(barrier, inc=1, device_id=peer, device_id_type=MESH)

    lines = []
    for k, value in enumerate((bias, gain, beta)):
        lines.append(pltpu.make_async_copy(value, rows_of.at[k, 0], row_sems.at[k]))
        lines[-1].start()
    loads = []
    for k, (source, target) in enumerate(tap_rows()):
        loads.append(
            pltpu.make_async_copy(
                conv_weight.at[pl.ds(source, CL)], packed.at[pl.ds(target, CL)], weight_sems.at[k]
            )
        )
        loads[-1].start()
    filled = 3 * LANES + 3 * CL
    packed[filled:, :] = jnp.zeros((DEEP - filled, D), jnp.bfloat16)

    lane16 = lax.broadcasted_iota(jnp.int32, (CL, LANES), 1)
    chan = lax.broadcasted_iota(jnp.int32, (CL, LANES), 0)
    for half in range(2):
        total = jnp.zeros((frames * cols, LANES), jnp.float32)
        for y in range(8):
            pick = jnp.where(lane16 == chan + y * CL, 1.0, 0.0).astype(jnp.bfloat16)
            line = latent[:, half * 8 + y].reshape(frames * cols, CL)
            total = total + jnp.dot(line, pick, preferred_element_type=jnp.float32)
        lanes = slice((1 + half) * LANES, (2 + half) * LANES)
        field[:, 8:24, lanes] = total.reshape(frames, cols, LANES)

    pl.semaphore_wait(barrier, len(peers))

    first, last, both = (8, 8), (16, 8), (8, 16)
    x_low, x_high = (0, 8), (24, 8)
    y_first, y_last, y_both = (LANES, LANES), (2 * LANES, LANES), (LANES, 2 * LANES)
    y_low, y_high = (0, LANES), (3 * LANES, LANES)
    plan = [
        ({"col": right}, last, y_both, x_low, y_both),
        ({"col": left}, first, y_both, x_high, y_both),
        ({"row": down}, both, y_last, both, y_low),
        ({"row": up}, both, y_first, both, y_high),
        (corners[0], last, y_last, x_low, y_low),
        (corners[1], first, y_last, x_high, y_low),
        (corners[2], last, y_first, x_low, y_high),
        (corners[3], first, y_first, x_high, y_high),
    ]
    halos = []
    for k, (peer, sx, sy, dx, dy) in enumerate(plan):
        halos.append(
            pltpu.make_async_remote_copy(
                src_ref=field.at[:, pl.ds(*sx), pl.ds(*sy)],
                dst_ref=field.at[:, pl.ds(*dx), pl.ds(*dy)],
                send_sem=halo_send.at[k],
                recv_sem=halo_recv.at[k],
                device_id=peer,
                device_id_type=MESH,
            )
        )
        halos[-1].start()

    move_row = signed_shift(shifts[1], WH)
    move_col = signed_shift(shifts[2], WW)
    way[0] = jnp.where(shifts[1] > HALF, 2, 0) + jnp.where(shifts[2] > HALF, 1, 0)
    for copy in lines:
        copy.wait()
    for copy in halos:
        copy.wait()

    turned = pltpu.roll(field[...].reshape(frames * 32, DEEP), 400 - 16 * move_row, 1)
    turned = turned[:, : 3 * LANES].reshape(frames, 32, 3 * LANES)
    moved[...] = pltpu.roll(turned, 25 - move_col, 1)

    lane = lax.broadcasted_iota(jnp.int32, (frames * cols, LANES), 1)
    place = lax.broadcasted_iota(jnp.int32, (frames * cols, LANES), 0) % cols
    wide_cols, wide_rows = n_col * cols, n_row * rows
    at_col = lax.rem(me_col * cols + move_col + place + wide_cols, wide_cols)
    pieces = []
    for c in range(3):
        piece = moved[:, c : c + cols, :].reshape(frames * cols, 3 * LANES)
        parts = [piece[:, k * LANES : (k + 1) * LANES] for k in range(3)]
        if c == 0:
            parts = [jnp.where(at_col == 0, 0.0, p) for p in parts]
        if c == 2:
            parts = [jnp.where(at_col == wide_cols - 1, 0.0, p) for p in parts]
        pieces.append(parts)
    row_tap = (lane // CL) % 3

    def line_of(y):
        at_row = lax.rem(me_row * rows + move_row + y + wide_rows, wide_rows)
        turned = []
        for c in range(3):
            k, start = divmod(y * CL, LANES)
            value = pieces[c][k]
            if start + 48 > LANES:
                value = jnp.where(lane < start + 48 - LANES, pieces[c][k + 1], value)
            turned.append(pltpu.roll(value, (c * 48 - start) % LANES, 1))
        full = jnp.where(lane < 48, turned[0], jnp.where(lane < 96, turned[1], turned[2]))
        gone = jnp.where(at_row == 0, 0, -1)
        full = jnp.where(row_tap == gone, 0.0, full)
        gone = jnp.where(at_row == wide_rows - 1, 2, -1)
        full = jnp.where(row_tap == gone, 0.0, full)
        some = jnp.where(lane < jnp.where(at_row == wide_rows - 1, 0, CL), turned[2], 0.0)
        return full, some

    for y in range(0, rows, 2):
        fulls, somes = zip(*[line_of(y + k) for k in range(2)])
        a, h = divmod(y, WH)
        full = jnp.concatenate([v.reshape(frames, cols // WW, WW, LANES) for v in fulls], 2)
        some = jnp.concatenate([v.reshape(frames, cols // WW, WW, LANES) for v in somes], 2)
        for b in range(cols // WW):
            lines16 = slice(((a * (cols // WW)) + b) * 64 + h * WW, ((a * (cols // WW)) + b) * 64 + h * WW + 16)
            wide[:, lines16, :] = full[:, b].astype(jnp.bfloat16)
            thin[:, lines16, :] = some[:, b]

    for t in range(frames):
        frame = lax.rem(shifts[0] + t, frames)
        sources = [jnp.maximum(frame - 2, 0), jnp.maximum(frame - 1, 0), frame]
        rest = thin[sources[0]]
        rest = rest + pltpu.roll(thin[sources[1]], CL, 1)
        rest = rest + pltpu.roll(thin[sources[2]], 2 * CL, 1)
        blocks = [wide[f] for f in sources] + [rest.astype(jnp.bfloat16)]
        for w in range(rows * cols // 64):
            a, b = divmod(w, cols // WW)
            window = (a * (frames // WT) + t // WT) * (cols // WW) + b
            start = window * CELLS + (t % WT) * 64
            for k in range(4):
                stacked[start : start + 64, k * LANES : (k + 1) * LANES] = blocks[k][w * 64 : w * 64 + 64]

    for copy in loads:
        copy.wait()
    keep = pltpu.make_async_copy(packed, packed_out, out_sem)
    keep.start()

    total = frames * rows * cols
    sums[...] = jnp.zeros_like(sums)
    squares[...] = jnp.zeros_like(squares)

    @pl.loop(0, total // 256)
    def _(i):
        block = stacked[pl.ds(pl.multiple_of(i * 256, 256), 256), :]
        for n in range(0, D, 512):
            hidden = jnp.dot(block, packed[:, n : n + 512], preferred_element_type=jnp.float32)
            grouped = hidden.reshape(32, 8, 512)
            sums[:, n : n + 512] += jnp.sum(grouped, axis=0)
            squares[:, n : n + 512] += jnp.sum(grouped * grouped, axis=0)

    first_sums, second_sums = sums[...], squares[...]
    for by in (4, 2, 1):
        first_sums = first_sums + pltpu.roll(first_sums, by, 0)
        second_sums = second_sums + pltpu.roll(second_sums, by, 0)
    second_sums = second_sums + rows_of[0] * (2.0 * first_sums + total * rows_of[0])
    first_sums = first_sums + total * rows_of[0]

    sub = lax.broadcasted_iota(jnp.int32, (8, LANES), 0)
    lane8 = lax.broadcasted_iota(jnp.int32, (8, LANES), 1)
    width = D // GROUPS
    segments = []
    for i in range(SPAN // LANES):
        value = jnp.zeros((8, LANES), jnp.float32)
        for s in range(D // SPAN):
            lanes = slice(s * SPAN + i * LANES, s * SPAN + (i + 1) * LANES)
            value = jnp.where(sub == s, first_sums[:, lanes], value)
            value = jnp.where(sub == s + 4, second_sums[:, lanes], value)
        segments.append(value)
    table = jnp.zeros((8, LANES), jnp.float32)
    for j in range(SPAN // width):
        low, high = j * width, (j + 1) * width
        column = jnp.zeros((8, LANES), jnp.float32)
        for i in range(SPAN // LANES):
            start = i * LANES
            if low < start + LANES and high > start:
                inside = (lane8 >= low - start) & (lane8 < high - start)
                column = column + jnp.where(inside, segments[i], 0.0)
        table = jnp.where(lane8 == j, jnp.sum(column, axis=1, keepdims=True), table)

    part[0] = table
    slot = 0
    for phase, group in enumerate(groups):
        copies = []
        for k, peer in enumerate(group):
            copies.append(
                pltpu.make_async_remote_copy(
                    src_ref=part.at[phase],
                    dst_ref=arrived.at[slot + k],
                    send_sem=sum_send.at[slot + k],
                    recv_sem=sum_recv.at[slot + k],
                    device_id=peer,
                    device_id_type=MESH,
                )
            )
            copies[-1].start()
        table = part[phase]
        for k, copy in enumerate(copies):
            copy.wait()
            table = table + arrived[slot + k]
        part[phase + 1] = table
        slot += len(group)

    count = total * n_row * n_col * width
    mean = table * (1.0 / count)
    var = pltpu.roll(mean, 4, 0) - mean * mean
    scale = lax.rsqrt(var + EPS)
    for i in range(SPAN // LANES):
        mean_here = jnp.zeros((8, LANES), jnp.float32)
        scale_here = jnp.zeros((8, LANES), jnp.float32)
        for j in range(SPAN // width):
            low, high = j * width - i * LANES, (j + 1) * width - i * LANES
            if low < LANES and high > 0:
                inside = (lane8 >= low) & (lane8 < high)
                mean_here = jnp.where(inside, mean[:, j : j + 1], mean_here)
                scale_here = jnp.where(inside, scale[:, j : j + 1], scale_here)
        for s in range(D // SPAN):
            lanes = slice(s * SPAN + i * LANES, s * SPAN + (i + 1) * LANES)
            means[:, lanes] = mean_here[s : s + 1]
            scales[:, lanes] = scale_here[s : s + 1]
    steep = 0.5 * scales[...] * rows_of[1]
    slope[...] = steep
    offset[...] = (rows_of[0] - means[...]) * steep + 0.5 * rows_of[2]
    keep.wait()


def front(dims, latent, conv_weight, conv_bias, norm_gain, norm_bias, shifts):
    frames, rows, cols = dims
    total = frames * rows * cols
    count = lax.axis_size("row") + lax.axis_size("col") - 2
    vmem = pl.BlockSpec(memory_space=pltpu.VMEM)
    hbm = pl.BlockSpec(memory_space=pl.ANY)
    smem = pl.BlockSpec(memory_space=pltpu.SMEM)
    return pl.pallas_call(
        functools.partial(front_kernel, dims),
        out_shape=[
            jax.ShapeDtypeStruct((total, DEEP), jnp.bfloat16),
            jax.ShapeDtypeStruct((DEEP, D), jnp.bfloat16),
            jax.ShapeDtypeStruct((1, D), jnp.float32),
            jax.ShapeDtypeStruct((1, D), jnp.float32),
            jax.ShapeDtypeStruct((1,), jnp.int32),
        ],
        in_specs=[vmem, hbm, hbm, hbm, hbm, smem],
        out_specs=[vmem, hbm, vmem, vmem, smem],
        scratch_shapes=[
            pltpu.VMEM((frames, 32, DEEP), jnp.float32),
            pltpu.VMEM((frames, 32, 3 * LANES), jnp.float32),
            pltpu.VMEM((frames, rows * cols, LANES), jnp.bfloat16),
            pltpu.VMEM((frames, rows * cols, LANES), jnp.float32),
            pltpu.VMEM((DEEP, D), jnp.bfloat16),
            pltpu.VMEM((8, D), jnp.float32),
            pltpu.VMEM((8, D), jnp.float32),
            pltpu.VMEM((1, D), jnp.float32),
            pltpu.VMEM((1, D), jnp.float32),
            pltpu.VMEM((3, 1, D), jnp.float32),
            pltpu.VMEM((3, 8, LANES), jnp.float32),
            pltpu.VMEM((count, 8, LANES), jnp.float32),
            pltpu.SemaphoreType.DMA((27,)),
            pltpu.SemaphoreType.DMA((8,)),
            pltpu.SemaphoreType.DMA((8,)),
            pltpu.SemaphoreType.DMA((count,)),
            pltpu.SemaphoreType.DMA((count,)),
            pltpu.SemaphoreType.DMA,
            pltpu.SemaphoreType.DMA((3,)),
        ],
        compiler_params=pltpu.CompilerParams(
            collective_id=1, has_side_effects=True, vmem_limit_bytes=32 * 1024 * 1024
        ),
    )(latent, conv_weight, conv_bias, norm_gain, norm_bias, shifts)


def per_device(latent, conv_weight, conv_bias, norm_gain, norm_bias, qkv_weight, shifts):
    dims = (latent.shape[0], latent.shape[1], latent.shape[2])
    stacked, packed, slope, offset, way = front(
        dims, latent, conv_weight, conv_bias, norm_gain, norm_bias, shifts
    )
    branches = [functools.partial(attend, dims, way) for way in range(4)]
    results = lax.switch(way[0], branches, stacked, packed, slope, offset, qkv_weight)
    return place(dims, shifts, *results)


def solution(mesh):
    in_specs = (P(None, "row", "col", None), P(), P(), P(), P(), P(), P())
    out_specs = P(None, "row", "col", None)
    return jax.shard_map(
        per_device, mesh=mesh, in_specs=in_specs, out_specs=out_specs, check_vma=False
    )
```

```python
import functools
import math

import jax
import jax.numpy as jnp
from jax import lax
from jax.experimental import pallas as pl
from jax.experimental.pallas import tpu as pltpu
from jax.sharding import PartitionSpec as P

CL = 16
GROUPS = 32
D = 2560
HEADS = 10
HD = 128
WT = 2
WH = 8
WW = 8
HALF = 4


def signed_shift(shift, window):
    return jnp.where(shift <= HALF, shift, shift - window)


CELLS = WT * WH * WW
PAIR = 2 * HD


STEPS = HEADS // 2


def attend_kernel(
    dims,
    way,
    stacked,
    conv_weight,
    slope,
    offset,
    qkv_weight,
    own_out,
    row_out,
    col_out,
    corner_out,
    feat,
    qkv,
    weights,
    own,
    edge,
    weight_sems,
    own_sems,
    row_send,
    row_recv,
    col_send,
    col_recv,
    corner_send,
    corner_recv,
):
    frames, rows, cols = dims
    total = frames * rows * cols
    step = pl.program_id(0)
    n_row, n_col = lax.axis_size("row"), lax.axis_size("col")
    me_row, me_col = lax.axis_index("row"), lax.axis_index("col")
    to_row = {"row": lax.rem(me_row + (n_row - 1 if way else 1), n_row)}
    from_row = {"row": lax.rem(me_row + (1 if way else n_row - 1), n_row)}
    sides = [{"col": lax.rem(me_col + k, n_col)} for k in (1, n_col - 1)]
    across, deep = cols // WW, frames // WT
    row_edge = 0 if way else rows // WH - 1
    order = [row_edge] + [a for a in range(rows // WH) if a != row_edge]

    def sends(p, a):
        copies = []
        for side, peer in enumerate(sides):
            copies.append(
                pltpu.make_async_remote_copy(
                    src_ref=edge.at[side, p, a],
                    dst_ref=col_out.at[side, p, a],
                    send_sem=col_send.at[side, p, a],
                    recv_sem=col_recv.at[side, p, a],
                    device_id=peer,
                    device_id_type=MESH,
                )
            )
        if a == row_edge:
            lines = pl.ds(0 if way else 32, 32)
            copies.append(
                pltpu.make_async_remote_copy(
                    src_ref=own.at[p, pl.ds(a * across, across), :, lines],
                    dst_ref=row_out.at[p],
                    send_sem=row_send.at[p],
                    recv_sem=row_recv.at[p],
                    device_id=to_row,
                    device_id_type=MESH,
                )
            )
            lines = pl.ds(0 if way else 16, 16)
            for side, peer in enumerate(sides):
                copies.append(
                    pltpu.make_async_remote_copy(
                        src_ref=edge.at[side, p, a, :, lines],
                        dst_ref=corner_out.at[side, p],
                        send_sem=corner_send.at[side, p],
                        recv_sem=corner_recv.at[side, p],
                        device_id=to_row | peer,
                        device_id_type=MESH,
                    )
                )
        return copies

    def keep(p, a):
        rows_of = pl.ds(a * across, across)
        return pltpu.make_async_copy(own.at[p, rows_of], own_out.at[p, rows_of], own_sems.at[p, a])

    def loads(p):
        slot = lax.rem(p, 2)
        copies = []
        for j in range(3):
            columns = pl.ds(pl.multiple_of((j * STEPS + p) * PAIR, PAIR), PAIR)
            copies.append(
                pltpu.make_async_copy(
                    qkv_weight.at[:, columns], weights.at[slot, j], weight_sems.at[slot, j]
                )
            )
        return copies

    part = total // len(order)

    def lines_of(a):
        return slice(a * part, (a + 1) * part)

    def project(p, j, lines=slice(0, total)):
        slot = lax.rem(p, 2)
        qkv[slot, lines, j * PAIR : (j + 1) * PAIR] = jnp.dot(
            feat[lines, :], weights[slot, j], preferred_element_type=jnp.float32
        ).astype(jnp.bfloat16)

    def features(lines, places):
        block = stacked[lines, :]
        for k in places:
            n = slice(k * PAIR, (k + 1) * PAIR)
            hidden = jnp.dot(block, conv_weight[:, n], preferred_element_type=jnp.float32)
            half = hidden * slope[:, n] + offset[:, n]
            feat[lines, n] = (half + half * jnp.tanh(half)).astype(jnp.bfloat16)

    sub = lax.broadcasted_iota(jnp.int32, (WH // 2, WW, HD), 1)

    def attention(p):
        source = lax.rem(p, 2)

        def part(item, j):
            window, head = item
            first = j * PAIR + head * HD
            return qkv[source, window * CELLS : (window + 1) * CELLS, first : first + HD]

        def score(item):
            return lax.dot_general(
                part(item, 0), part(item, 1), (((1,), (1,)), ((), ())), preferred_element_type=jnp.float32
            )

        def softmax(scores):
            most = [jnp.max(x, axis=-1, keepdims=True) for x in scores]
            powers = [
                jnp.exp2((x - m) * (math.log2(math.e) / HD**0.5)) for x, m in zip(scores, most)
            ]
            sums = [jnp.sum(x, axis=-1, keepdims=True) for x in powers]
            return [(x * (1.0 / t)).astype(jnp.bfloat16) for x, t in zip(powers, sums)]

        def items(a):
            return [(w, head) for head in range(2) for w in range(a * deep * across, (a + 1) * deep * across)]

        def store(a, item, result):
            window, head = item
            t2, b = divmod(window - a * deep * across, across)
            lanes = slice(head * HD, (head + 1) * HD)
            halves = result.reshape(WT, WH * WW, HD)
            for t in range(WT):
                own[p, a * across + b, t2 * WT + t, :, lanes] = halves[t].astype(jnp.bfloat16)
            lines = result.reshape(WT, WH // 2, 2, WW, HD)
            for side in range(2):
                if b != (0 if side else across - 1):
                    continue
                for t in range(WT):
                    even, odd = lines[t, :, 0], lines[t, :, 1]
                    if side:
                        packed = jnp.where(sub < 4, even, pltpu.roll(odd, 4, 1))
                    else:
                        packed = jnp.where(sub < 4, pltpu.roll(even, 4, 1), odd)
                    edge[side, p, a, t2 * WT + t, :, lanes] = packed.reshape(WH * HALF, HD).astype(
                        jnp.bfloat16
                    )

        def apply(names, probs):
            return [
                jnp.dot(x, part(item, 2), preferred_element_type=jnp.float32)
                for item, x in zip(names, probs)
            ]

        return items, score, softmax, apply, store

    def send(p, a):
        for copy in sends(p, a):
            copy.start()
        keep(p, a).start()

    def run(p, jobs):
        items, score, softmax, apply, store = attention(p)
        waiting = [score(item) for item in items(order[0])]
        for k, a in enumerate(order):
            jobs[k]()
            results = apply(items(a), softmax(waiting))
            if k + 1 < len(order):
                waiting = [score(item) for item in items(order[k + 1])]
            for item, result in zip(items(a), results):
                store(a, item, result)
        jobs[len(order)]()
        for a in order:
            send(p, a)

    last = STEPS - 1
    ahead, behind = lines_of(order[0]), lines_of(order[1])

    @pl.when(step == 0)
    def _():
        for p in range(2):
            for copy in loads(p):
                copy.start()
        barrier = pltpu.get_barrier_semaphore()
        for peer in [from_row] + sides + [from_row | side for side in sides]:
            pl.semaphore_signal(barrier, inc=1, device_id=peer, device_id_type=MESH)
        features(ahead, range(D // PAIR))
        for copy in loads(0):
            copy.wait()
        for j, places in enumerate((range(4), range(4, 7), range(7, D // PAIR))):
            features(behind, places)
            project(0, j, ahead)
        for j in range(3):
            project(0, j, behind)
        pl.semaphore_wait(barrier, 5)

    @pl.when((step > 0) & (step < last))
    def _():
        for copy in loads(step):
            copy.wait()
        for copy in loads(step + 1):
            copy.start()
        run(step - 1, [functools.partial(project, step, j) for j in range(3)])

    @pl.when(step == last)
    def _():
        for copy in loads(last):
            copy.wait()
        run(last - 1, [functools.partial(project, last, j, ahead) for j in range(3)])

    @pl.when(step == STEPS)
    def _():
        items, score, softmax, apply, store = attention(last)
        waiting = [score(item) for item in items(order[0])]
        project(last, 0, behind)
        results = apply(items(order[0]), softmax(waiting))
        for item, result in zip(items(order[0]), results):
            store(order[0], item, result)
        send(last, order[0])
        project(last, 1, behind)
        waiting = [score(item) for item in items(order[1])]
        project(last, 2, behind)
        results = apply(items(order[1]), softmax(waiting))
        for item, result in zip(items(order[1]), results):
            store(order[1], item, result)
        send(last, order[1])

        @pl.loop(0, STEPS)
        def _(p):
            for a in order:
                for copy in sends(p, a):
                    copy.wait()
                keep(p, a).wait()


def attend(dims, way, stacked, conv_weight, slope, offset, qkv_weight):
    frames, rows, cols = dims
    total = frames * rows * cols
    quarters = (rows // WH) * (cols // WW)

    def whole(x):
        return pl.BlockSpec(x.shape, lambda h: (0,) * x.ndim, pipeline_mode=pl.Buffered(1))

    hbm = pl.BlockSpec(memory_space=pl.ANY)
    own = (STEPS, quarters, frames, WH * WW, PAIR)
    row = (STEPS, cols // WW, frames, HALF * WW, PAIR)
    col = (2, STEPS, rows // WH, frames, HALF * WH, PAIR)
    corner = (2, STEPS, frames, HALF * HALF, PAIR)
    dma = pltpu.SemaphoreType.DMA
    return pl.pallas_call(
        functools.partial(attend_kernel, dims, way),
        grid=(STEPS + 1,),
        out_shape=[jax.ShapeDtypeStruct(shape, jnp.bfloat16) for shape in (own, row, col, corner)],
        in_specs=[
            whole(stacked),
            whole(conv_weight),
            whole(slope),
            whole(offset),
            hbm,
        ],
        out_specs=[hbm] * 4,
        scratch_shapes=[
            pltpu.VMEM((total, D), jnp.bfloat16),
            pltpu.VMEM((2, total, 3 * PAIR), jnp.bfloat16),
            pltpu.VMEM((2, 3, D, PAIR), jnp.bfloat16),
            pltpu.VMEM(own, jnp.bfloat16),
            pltpu.VMEM(col, jnp.bfloat16),
            dma((2, 3)),
            dma((STEPS, rows // WH)),
            dma((STEPS,)),
            dma((STEPS,)),
            dma((2, STEPS, rows // WH)),
            dma((2, STEPS, rows // WH)),
            dma((2, STEPS)),
            dma((2, STEPS)),
        ],
        compiler_params=pltpu.CompilerParams(
            collective_id=2 + way, has_side_effects=True, vmem_limit_bytes=60 * 1024 * 1024
        ),
    )(stacked, conv_weight, slope, offset, qkv_weight)


def place_kernel(
    dims, shifts, own_in, row_in, col_in, corner_in, result, own, row, col, corner, out, field, in_sems, out_sems
):
    frames, rows, cols = dims
    across = cols // WW
    move_row = signed_shift(shifts[1], WH)
    move_col = signed_shift(shifts[2], WW)
    high, blocks = rows + HALF, cols // WW + 1
    turn = lax.rem(move_col + blocks * WW, blocks * WW)
    jump, slide = turn // WW, lax.rem(turn, WW)
    later = lax.broadcasted_iota(jnp.int32, (WW, PAIR), 0) >= slide

    def spread(value):
        lines = value.astype(jnp.float32).reshape(-1, 8, PAIR)
        low = lax.broadcasted_iota(jnp.int32, lines.shape, 1) < HALF
        other = pltpu.roll(lines, HALF, 1)
        pair = jnp.stack([jnp.where(low, lines, other), jnp.where(low, other, lines)], 1)
        return pair.reshape(-1, 8, PAIR)

    side = jnp.where(shifts[2] > HALF, 1, 0)

    def loads(t):
        pairs = ((own_in, own), (row_in, row), (col_in.at[side], col))
        copies = [
            pltpu.make_async_copy(x.at[:, :, t], y.at[:, :, t], in_sems.at[t, k])
            for k, (x, y) in enumerate(pairs)
        ]
        copies.append(pltpu.make_async_copy(corner_in.at[side, :, t], corner.at[:, t], in_sems.at[t, 3]))
        return copies

    def leave(t):
        frame = lax.rem(shifts[0] + t, frames)
        return pltpu.make_async_copy(out.at[t], result.at[frame], out_sems.at[t])

    for t in range(frames):
        for copy in loads(t):
            copy.start()

    @pl.loop(0, frames)
    def _(t):
        for copy in loads(t):
            copy.wait()
        for p in range(STEPS):
            for a in range(rows // WH):
                for b in range(across):
                    value = own[p, a * across + b, t].astype(jnp.float32)
                    field[p, a * WH : (a + 1) * WH, b] = value.reshape(WH, WW, PAIR)
                field[p, a * WH : (a + 1) * WH, across] = spread(col[p, a, t])
            for b in range(across):
                value = row[p, b, t].astype(jnp.float32)
                field[p, rows:, b] = value.reshape(HALF, WW, PAIR)
            field[p, rows:, across] = spread(corner[p, t])
            lanes = slice(p * PAIR, (p + 1) * PAIR)
            for y in range(rows):
                line = lax.rem(y - move_row + high, high)
                turned = [
                    pltpu.roll(field[p, line, lax.rem(k - jump + 2 * blocks, blocks)], slide, 0)
                    for k in range(-1, across)
                ]
                pieces = [jnp.where(later, turned[k + 1], turned[k]) for k in range(across)]
                out[t, y, :, lanes] = jnp.concatenate(pieces, 0).astype(jnp.bfloat16)
        leave(t).start()

    for t in range(frames):
        leave(t).wait()


def place(dims, shifts, own, row, col, corner):
    frames, rows, cols = dims
    hbm = pl.BlockSpec(memory_space=pl.ANY)
    shape = (frames, rows, cols, HEADS * HD)
    shapes = (own.shape, row.shape, col.shape[1:], corner.shape[1:])
    scratch = [pltpu.VMEM(x, jnp.bfloat16) for x in shapes]
    return pl.pallas_call(
        functools.partial(place_kernel, dims),
        in_specs=[pl.BlockSpec(memory_space=pltpu.SMEM)] + [hbm] * 4,
        out_specs=hbm,
        out_shape=jax.ShapeDtypeStruct(shape, jnp.bfloat16),
        scratch_shapes=scratch
        + [
            pltpu.VMEM(shape, jnp.bfloat16),
            pltpu.VMEM((STEPS, rows + HALF, cols // WW + 1, WW, PAIR), jnp.float32),
            pltpu.SemaphoreType.DMA((frames, 4)),
            pltpu.SemaphoreType.DMA((frames,)),
        ],
        compiler_params=pltpu.CompilerParams(vmem_limit_bytes=60 * 1024 * 1024),
    )(shifts, own, row, col, corner)


MESH = pl.DeviceIdType.MESH
LANES = 128
TAPS = 9
DEEP = 4 * LANES
SPAN = 640
EPS = 1e-05


def front_kernel(
    dims,
    latent,
    conv_weight,
    bias,
    gain,
    beta,
    shifts,
    stacked,
    packed_out,
    slope,
    offset,
    way,
    field,
    moved,
    wide,
    thin,
    packed,
    sums,
    squares,
    means,
    scales,
    rows_of,
    part,
    arrived,
    weight_sems,
    halo_send,
    halo_recv,
    sum_send,
    sum_recv,
    out_sem,
    row_sems,
):
    frames, rows, cols = dims
    n_row, n_col = lax.axis_size("row"), lax.axis_size("col")
    me_row, me_col = lax.axis_index("row"), lax.axis_index("col")
    down, up = lax.rem(me_row + 1, n_row), lax.rem(me_row + n_row - 1, n_row)
    right, left = lax.rem(me_col + 1, n_col), lax.rem(me_col + n_col - 1, n_col)

    groups = []
    for axis, me, count in (("col", me_col, n_col), ("row", me_row, n_row)):
        groups.append([{axis: lax.rem(me + k, count)} for k in range(1, count)])
    corners = [{"row": r, "col": c} for r in (down, up) for c in (right, left)]
    peers = groups[0] + groups[1] + corners
    barrier = pltpu.get_barrier_semaphore()
    for peer in peers:
        pl.semaphore_signal(barrier, inc=1, device_id=peer, device_id_type=MESH)

    lines = []
    for k, value in enumerate((bias, gain, beta)):
        lines.append(pltpu.make_async_copy(value, rows_of.at[k, 0], row_sems.at[k]))
        lines[-1].start()
    lane16 = lax.broadcasted_iota(jnp.int32, (CL, LANES), 1)
    chan = lax.broadcasted_iota(jnp.int32, (CL, LANES), 0)
    for half in range(2):
        total = jnp.zeros((frames * cols, LANES), jnp.float32)
        for y in range(8):
            pick = jnp.where(lane16 == chan + y * CL, 1.0, 0.0).astype(jnp.bfloat16)
            line = latent[:, half * 8 + y].reshape(frames * cols, CL)
            total = total + jnp.dot(line, pick, preferred_element_type=jnp.float32)
        lanes = slice((1 + half) * LANES, (2 + half) * LANES)
        field[:, 8:24, lanes] = total.reshape(frames, cols, LANES)

    pl.semaphore_wait(barrier, len(peers))

    first, last, both = (8, 8), (16, 8), (8, 16)
    x_low, x_high = (0, 8), (24, 8)
    y_first, y_last, y_both = (LANES, LANES), (2 * LANES, LANES), (LANES, 2 * LANES)
    y_low, y_high = (0, LANES), (3 * LANES, LANES)
    plan = [
        ({"col": right}, last, y_both, x_low, y_both),
        ({"col": left}, first, y_both, x_high, y_both),
        ({"row": down}, both, y_last, both, y_low),
        ({"row": up}, both, y_first, both, y_high),
        (corners[0], last, y_last, x_low, y_low),
        (corners[1], first, y_last, x_high, y_low),
        (corners[2], last, y_first, x_low, y_high),
        (corners[3], first, y_first, x_high, y_high),
    ]
    halos = []
    for k, (peer, sx, sy, dx, dy) in enumerate(plan):
        halos.append(
            pltpu.make_async_remote_copy(
                src_ref=field.at[:, pl.ds(*sx), pl.ds(*sy)],
                dst_ref=field.at[:, pl.ds(*dx), pl.ds(*dy)],
                send_sem=halo_send.at[k],
                recv_sem=halo_recv.at[k],
                device_id=peer,
                device_id_type=MESH,
            )
        )
        halos[-1].start()

    blocks = pl.ds(0, 3)
    loads = [
        pltpu.make_async_copy(conv_weight.at[:, :, 0], packed.at[blocks, pl.ds(0, 3)], weight_sems.at[0]),
        pltpu.make_async_copy(conv_weight.at[:, :, 1], packed.at[blocks, pl.ds(3, 3)], weight_sems.at[1]),
        pltpu.make_async_copy(
            conv_weight.at[:, pl.ds(0, 2), 2], packed.at[blocks, pl.ds(6, 2)], weight_sems.at[2]
        ),
        pltpu.make_async_copy(conv_weight.at[:, 2, 2], packed.at[3, pl.ds(0, 3)], weight_sems.at[3]),
    ]
    for copy in loads:
        copy.start()
    packed[3, 3:] = jnp.zeros((5, CL, D), jnp.bfloat16)

    move_row = signed_shift(shifts[1], WH)
    move_col = signed_shift(shifts[2], WW)
    way[0] = jnp.where(shifts[1] > HALF, 1, 0)
    for copy in lines:
        copy.wait()
    for copy in halos:
        copy.wait_recv()

    turned = pltpu.roll(field[...].reshape(frames * 32, DEEP), 400 - 16 * move_row, 1)
    turned = turned[:, : 3 * LANES].reshape(frames, 32, 3 * LANES)
    moved[...] = pltpu.roll(turned, 25 - move_col, 1)

    lane = lax.broadcasted_iota(jnp.int32, (frames * cols, LANES), 1)
    place = lax.broadcasted_iota(jnp.int32, (frames * cols, LANES), 0) % cols
    wide_cols, wide_rows = n_col * cols, n_row * rows
    at_col = lax.rem(me_col * cols + move_col + place + wide_cols, wide_cols)
    pieces = []
    for c in range(3):
        piece = moved[:, c : c + cols, :].reshape(frames * cols, 3 * LANES)
        parts = [piece[:, k * LANES : (k + 1) * LANES] for k in range(3)]
        if c == 0:
            parts = [jnp.where(at_col == 0, 0.0, p) for p in parts]
        if c == 2:
            parts = [jnp.where(at_col == wide_cols - 1, 0.0, p) for p in parts]
        pieces.append(parts)
    row_tap = (lane // CL) % 3

    def line_of(y):
        at_row = lax.rem(me_row * rows + move_row + y + wide_rows, wide_rows)
        turned = []
        for c in range(3):
            k, start = divmod(y * CL, LANES)
            value = pieces[c][k]
            if start + 48 > LANES:
                value = jnp.where(lane < start + 48 - LANES, pieces[c][k + 1], value)
            turned.append(pltpu.roll(value, (c * 48 - start) % LANES, 1))
        full = jnp.where(lane < 48, turned[0], jnp.where(lane < 96, turned[1], turned[2]))
        gone = jnp.where(at_row == 0, 0, -1)
        full = jnp.where(row_tap == gone, 0.0, full)
        gone = jnp.where(at_row == wide_rows - 1, 2, -1)
        full = jnp.where(row_tap == gone, 0.0, full)
        some = jnp.where(lane < jnp.where(at_row == wide_rows - 1, 0, CL), turned[2], 0.0)
        return full, some

    for y in range(0, rows, 2):
        fulls, somes = zip(*[line_of(y + k) for k in range(2)])
        a, h = divmod(y, WH)
        full = jnp.concatenate([v.reshape(frames, cols // WW, WW, LANES) for v in fulls], 2)
        some = jnp.concatenate([v.reshape(frames, cols // WW, WW, LANES) for v in somes], 2)
        for b in range(cols // WW):
            lines16 = slice(((a * (cols // WW)) + b) * 64 + h * WW, ((a * (cols // WW)) + b) * 64 + h * WW + 16)
            wide[:, lines16, :] = full[:, b].astype(jnp.bfloat16)
            thin[:, lines16, :] = some[:, b]

    for t in range(frames):
        frame = lax.rem(shifts[0] + t, frames)
        sources = [jnp.maximum(frame - 2, 0), jnp.maximum(frame - 1, 0), frame]
        rest = thin[sources[0]]
        rest = rest + pltpu.roll(thin[sources[1]], CL, 1)
        rest = rest + pltpu.roll(thin[sources[2]], 2 * CL, 1)
        blocks = [wide[f] for f in sources] + [rest.astype(jnp.bfloat16)]
        for w in range(rows * cols // 64):
            a, b = divmod(w, cols // WW)
            window = (a * (frames // WT) + t // WT) * (cols // WW) + b
            start = window * CELLS + (t % WT) * 64
            for k in range(4):
                stacked[start : start + 64, k * LANES : (k + 1) * LANES] = blocks[k][w * 64 : w * 64 + 64]

    for copy in loads:
        copy.wait()
    keep = pltpu.make_async_copy(packed, packed_out, out_sem)
    keep.start()

    total = frames * rows * cols
    for n in range(0, D, 256):
        weight = packed[:, :, :, n : n + 256].reshape(DEEP, 256)
        hidden = jnp.dot(stacked[...], weight, preferred_element_type=jnp.float32)
        grouped = hidden.reshape(total // 8, 8, 256)
        sums[:, n : n + 256] = jnp.sum(grouped, axis=0)
        squares[:, n : n + 256] = jnp.sum(grouped * grouped, axis=0)

    first_sums, second_sums = sums[...], squares[...]
    for by in (4, 2, 1):
        first_sums = first_sums + pltpu.roll(first_sums, by, 0)
        second_sums = second_sums + pltpu.roll(second_sums, by, 0)
    second_sums = second_sums + rows_of[0] * (2.0 * first_sums + total * rows_of[0])
    first_sums = first_sums + total * rows_of[0]

    sub = lax.broadcasted_iota(jnp.int32, (8, LANES), 0)
    lane8 = lax.broadcasted_iota(jnp.int32, (8, LANES), 1)
    width = D // GROUPS
    segments = []
    for i in range(SPAN // LANES):
        value = jnp.zeros((8, LANES), jnp.float32)
        for s in range(D // SPAN):
            lanes = slice(s * SPAN + i * LANES, s * SPAN + (i + 1) * LANES)
            value = jnp.where(sub == s, first_sums[:, lanes], value)
            value = jnp.where(sub == s + 4, second_sums[:, lanes], value)
        segments.append(value)
    table = jnp.zeros((8, LANES), jnp.float32)
    for j in range(SPAN // width):
        low, high = j * width, (j + 1) * width
        column = jnp.zeros((8, LANES), jnp.float32)
        for i in range(SPAN // LANES):
            start = i * LANES
            if low < start + LANES and high > start:
                inside = (lane8 >= low - start) & (lane8 < high - start)
                column = column + jnp.where(inside, segments[i], 0.0)
        table = jnp.where(lane8 == j, jnp.sum(column, axis=1, keepdims=True), table)

    part[0] = table
    slot = 0
    sent = list(halos)
    for phase, group in enumerate(groups):
        copies = []
        for k, peer in enumerate(group):
            copies.append(
                pltpu.make_async_remote_copy(
                    src_ref=part.at[phase],
                    dst_ref=arrived.at[slot + k],
                    send_sem=sum_send.at[slot + k],
                    recv_sem=sum_recv.at[slot + k],
                    device_id=peer,
                    device_id_type=MESH,
                )
            )
            copies[-1].start()
        sent += copies
        table = part[phase]
        for k, copy in enumerate(copies):
            copy.wait_recv()
            table = table + arrived[slot + k]
        part[phase + 1] = table
        slot += len(group)

    count = total * n_row * n_col * width
    mean = table * (1.0 / count)
    var = pltpu.roll(mean, 4, 0) - mean * mean
    scale = lax.rsqrt(var + EPS)
    for i in range(SPAN // LANES):
        mean_here = jnp.zeros((8, LANES), jnp.float32)
        scale_here = jnp.zeros((8, LANES), jnp.float32)
        for j in range(SPAN // width):
            low, high = j * width - i * LANES, (j + 1) * width - i * LANES
            if low < LANES and high > 0:
                inside = (lane8 >= low) & (lane8 < high)
                mean_here = jnp.where(inside, mean[:, j : j + 1], mean_here)
                scale_here = jnp.where(inside, scale[:, j : j + 1], scale_here)
        for s in range(D // SPAN):
            lanes = slice(s * SPAN + i * LANES, s * SPAN + (i + 1) * LANES)
            means[:, lanes] = mean_here[s : s + 1]
            scales[:, lanes] = scale_here[s : s + 1]
    steep = 0.5 * scales[...] * rows_of[1]
    slope[...] = steep
    offset[...] = (rows_of[0] - means[...]) * steep + 0.5 * rows_of[2]
    for copy in sent:
        copy.wait_send()
    keep.wait()


def front(dims, latent, conv_weight, conv_bias, norm_gain, norm_bias, shifts):
    frames, rows, cols = dims
    total = frames * rows * cols
    count = lax.axis_size("row") + lax.axis_size("col") - 2
    vmem = pl.BlockSpec(memory_space=pltpu.VMEM)
    hbm = pl.BlockSpec(memory_space=pl.ANY)
    smem = pl.BlockSpec(memory_space=pltpu.SMEM)
    return pl.pallas_call(
        functools.partial(front_kernel, dims),
        out_shape=[
            jax.ShapeDtypeStruct((total, DEEP), jnp.bfloat16),
            jax.ShapeDtypeStruct((4, 8, CL, D), jnp.bfloat16),
            jax.ShapeDtypeStruct((1, D), jnp.float32),
            jax.ShapeDtypeStruct((1, D), jnp.float32),
            jax.ShapeDtypeStruct((1,), jnp.int32),
        ],
        in_specs=[vmem, hbm, hbm, hbm, hbm, smem],
        out_specs=[vmem, hbm, vmem, vmem, smem],
        scratch_shapes=[
            pltpu.VMEM((frames, 32, DEEP), jnp.float32),
            pltpu.VMEM((frames, 32, 3 * LANES), jnp.float32),
            pltpu.VMEM((frames, rows * cols, LANES), jnp.bfloat16),
            pltpu.VMEM((frames, rows * cols, LANES), jnp.float32),
            pltpu.VMEM((4, 8, CL, D), jnp.bfloat16),
            pltpu.VMEM((8, D), jnp.float32),
            pltpu.VMEM((8, D), jnp.float32),
            pltpu.VMEM((1, D), jnp.float32),
            pltpu.VMEM((1, D), jnp.float32),
            pltpu.VMEM((3, 1, D), jnp.float32),
            pltpu.VMEM((3, 8, LANES), jnp.float32),
            pltpu.VMEM((count, 8, LANES), jnp.float32),
            pltpu.SemaphoreType.DMA((4,)),
            pltpu.SemaphoreType.DMA((8,)),
            pltpu.SemaphoreType.DMA((8,)),
            pltpu.SemaphoreType.DMA((count,)),
            pltpu.SemaphoreType.DMA((count,)),
            pltpu.SemaphoreType.DMA,
            pltpu.SemaphoreType.DMA((3,)),
        ],
        compiler_params=pltpu.CompilerParams(
            collective_id=1, has_side_effects=True, vmem_limit_bytes=60 * 1024 * 1024
        ),
    )(latent, conv_weight, conv_bias, norm_gain, norm_bias, shifts)


def per_device(latent, conv_weight, conv_bias, norm_gain, norm_bias, qkv_weight, shifts):
    dims = (latent.shape[0], latent.shape[1], latent.shape[2])
    stacked, packed, slope, offset, way = front(
        dims, latent, conv_weight.reshape(3, 3, 3, CL, D), conv_bias, norm_gain, norm_bias, shifts
    )
    packed = packed.reshape(DEEP, D)
    branches = [functools.partial(attend, dims, way) for way in range(2)]
    results = lax.switch(way[0], branches, stacked, packed, slope, offset, qkv_weight)
    return place(dims, shifts, *results)


def solution(mesh):
    in_specs = (P(None, "row", "col", None), P(), P(), P(), P(), P(), P())
    out_specs = P(None, "row", "col", None)
    return jax.shard_map(
        per_device, mesh=mesh, in_specs=in_specs, out_specs=out_specs, check_vma=False
    )
```

```python
import functools
import math

import jax
import jax.numpy as jnp
from jax import lax
from jax.experimental import pallas as pl
from jax.experimental.pallas import tpu as pltpu
from jax.sharding import PartitionSpec as P

CL = 16
GROUPS = 32
D = 2560
HEADS = 10
HD = 128
WT = 2
WH = 8
WW = 8
HALF = 4


def signed_shift(shift, window):
    return jnp.where(shift <= HALF, shift, shift - window)


CELLS = WT * WH * WW
PAIR = 2 * HD


MESH = pl.DeviceIdType.MESH
LANES = 128
TAPS = 9
DEEP = 4 * LANES
SPAN = 640
EPS = 1e-05
ONE_PHASE = 32


def prepare(
    dims,
    later_loads,
    latent,
    conv_weight,
    bias,
    gain,
    beta,
    shifts,
    conv,
    slope,
    offset,
    stacked,
    field,
    rim_cols,
    rim_rows,
    from_cols,
    from_rows,
    from_corners,
    moved,
    wide,
    thin,
    packed,
    sums,
    squares,
    means,
    scales,
    rows_of,
    part,
    arrived,
    weight_sems,
    halo_send,
    halo_recv,
    sum_send,
    sum_recv,
    row_sems,
):
    frames, rows, cols = dims
    n_row, n_col = lax.axis_size("row"), lax.axis_size("col")
    me_row, me_col = lax.axis_index("row"), lax.axis_index("col")
    down, up = lax.rem(me_row + 1, n_row), lax.rem(me_row + n_row - 1, n_row)
    right, left = lax.rem(me_col + 1, n_col), lax.rem(me_col + n_col - 1, n_col)

    by_row = [lax.rem(me_row + k, n_row) for k in range(n_row)]
    by_col = [lax.rem(me_col + k, n_col) for k in range(n_col)]
    corners = [{"row": r, "col": c} for r in (down, up) for c in (right, left)]
    if n_row * n_col <= ONE_PHASE:
        groups = [[{"row": r, "col": c} for r in by_row for c in by_col][1:]]
        peers = groups[0]
    else:
        groups = [[{"col": c} for c in by_col[1:]], [{"row": r} for r in by_row[1:]]]
        peers = groups[0] + groups[1] + corners
    barrier = pltpu.get_barrier_semaphore()
    for peer in peers:
        pl.semaphore_signal(barrier, inc=1, device_id=peer, device_id_type=MESH)

    lines = []
    for k, value in enumerate((bias, gain, beta)):
        lines.append(pltpu.make_async_copy(value, rows_of.at[k, 0], row_sems.at[k]))
        lines[-1].start()
    lane16 = lax.broadcasted_iota(jnp.int32, (CL, LANES), 1)
    chan = lax.broadcasted_iota(jnp.int32, (CL, LANES), 0)
    for half in range(2):
        total = jnp.zeros((frames * cols, LANES), jnp.float32)
        for y in range(8):
            pick = jnp.where(lane16 == chan + y * CL, 1.0, 0.0).astype(jnp.bfloat16)
            line = latent[:, half * 8 + y].reshape(frames * cols, CL)
            total = total + jnp.dot(line, pick, preferred_element_type=jnp.float32)
        lanes = slice((1 + half) * LANES, (2 + half) * LANES)
        field[:, 8:24, lanes] = total.reshape(frames, cols, LANES)

    rim_cols[0] = field[:, 16:24, LANES : 3 * LANES].reshape(frames // 2, 16, 2 * LANES).astype(jnp.bfloat16)
    rim_cols[1] = field[:, 8:16, LANES : 3 * LANES].reshape(frames // 2, 16, 2 * LANES).astype(jnp.bfloat16)
    rim_rows[0] = field[:, 8:24, 2 * LANES : 3 * LANES].astype(jnp.bfloat16)
    rim_rows[1] = field[:, 8:24, LANES : 2 * LANES].astype(jnp.bfloat16)

    pl.semaphore_wait(barrier, len(peers))

    low, high = pl.ds(0, LANES), pl.ds(LANES, LANES)
    plan = [
        ({"col": right}, rim_cols.at[0], from_cols.at[0]),
        ({"col": left}, rim_cols.at[1], from_cols.at[1]),
        ({"row": down}, rim_rows.at[0], from_rows.at[0]),
        ({"row": up}, rim_rows.at[1], from_rows.at[1]),
        (corners[0], rim_cols.at[0, :, :, high], from_corners.at[0]),
        (corners[1], rim_cols.at[1, :, :, high], from_corners.at[1]),
        (corners[2], rim_cols.at[0, :, :, low], from_corners.at[2]),
        (corners[3], rim_cols.at[1, :, :, low], from_corners.at[3]),
    ]
    halos = []
    for k, (peer, source, target) in enumerate(plan):
        halos.append(
            pltpu.make_async_remote_copy(
                src_ref=source,
                dst_ref=target,
                send_sem=halo_send.at[k],
                recv_sem=halo_recv.at[k],
                device_id=peer,
                device_id_type=MESH,
            )
        )
        halos[-1].start()

    blocks = pl.ds(0, 3)
    loads = [
        pltpu.make_async_copy(conv_weight.at[:, :, 0], packed.at[blocks, pl.ds(0, 3)], weight_sems.at[0]),
        pltpu.make_async_copy(conv_weight.at[:, :, 1], packed.at[blocks, pl.ds(3, 3)], weight_sems.at[1]),
        pltpu.make_async_copy(
            conv_weight.at[:, pl.ds(0, 2), 2], packed.at[blocks, pl.ds(6, 2)], weight_sems.at[2]
        ),
        pltpu.make_async_copy(conv_weight.at[:, 2, 2], packed.at[3, pl.ds(0, 3)], weight_sems.at[3]),
    ]
    for copy in loads:
        copy.start()
    packed[3, 3:] = jnp.zeros((5, CL, D), jnp.bfloat16)

    move_row = signed_shift(shifts[1], WH)
    move_col = signed_shift(shifts[2], WW)
    for copy in lines:
        copy.wait()
    for copy in halos:
        copy.wait_recv()
    wide_lanes = slice(LANES, 3 * LANES)
    for k, at in enumerate((slice(0, 8), slice(24, 32))):
        field[:, at, wide_lanes] = from_cols[k].astype(jnp.float32).reshape(frames, 8, 2 * LANES)
    for k, lanes in enumerate((slice(0, LANES), slice(3 * LANES, DEEP))):
        field[:, 8:24, lanes] = from_rows[k].astype(jnp.float32)
        for side, at in enumerate((slice(0, 8), slice(24, 32))):
            value = from_corners[2 * k + side].astype(jnp.float32)
            field[:, at, lanes] = value.reshape(frames, 8, LANES)

    turned = pltpu.roll(field[...].reshape(frames * 32, DEEP), 400 - 16 * move_row, 1)
    turned = turned[:, : 3 * LANES].reshape(frames, 32, 3 * LANES)
    moved[...] = pltpu.roll(turned, 25 - move_col, 1)

    lane = lax.broadcasted_iota(jnp.int32, (frames * cols, LANES), 1)
    place = lax.broadcasted_iota(jnp.int32, (frames * cols, LANES), 0) % cols
    wide_cols, wide_rows = n_col * cols, n_row * rows
    at_col = lax.rem(me_col * cols + move_col + place + wide_cols, wide_cols)
    pieces = []
    for c in range(3):
        piece = moved[:, c : c + cols, :].reshape(frames * cols, 3 * LANES)
        parts = [piece[:, k * LANES : (k + 1) * LANES] for k in range(3)]
        if c == 0:
            parts = [jnp.where(at_col == 0, 0.0, p) for p in parts]
        if c == 2:
            parts = [jnp.where(at_col == wide_cols - 1, 0.0, p) for p in parts]
        pieces.append(parts)
    row_tap = (lane // CL) % 3

    def line_of(y):
        at_row = lax.rem(me_row * rows + move_row + y + wide_rows, wide_rows)
        turned = []
        for c in range(3):
            k, start = divmod(y * CL, LANES)
            value = pieces[c][k]
            if start + 48 > LANES:
                value = jnp.where(lane < start + 48 - LANES, pieces[c][k + 1], value)
            turned.append(pltpu.roll(value, (c * 48 - start) % LANES, 1))
        full = jnp.where(lane < 48, turned[0], jnp.where(lane < 96, turned[1], turned[2]))
        gone = jnp.where(at_row == 0, 0, -1)
        full = jnp.where(row_tap == gone, 0.0, full)
        gone = jnp.where(at_row == wide_rows - 1, 2, -1)
        full = jnp.where(row_tap == gone, 0.0, full)
        some = jnp.where(lane < jnp.where(at_row == wide_rows - 1, 0, CL), turned[2], 0.0)
        return full, some

    for y in range(0, rows, 2):
        fulls, somes = zip(*[line_of(y + k) for k in range(2)])
        a, h = divmod(y, WH)
        full = jnp.concatenate([v.reshape(frames, cols // WW, WW, LANES) for v in fulls], 2)
        some = jnp.concatenate([v.reshape(frames, cols // WW, WW, LANES) for v in somes], 2)
        for b in range(cols // WW):
            lines16 = slice(((a * (cols // WW)) + b) * 64 + h * WW, ((a * (cols // WW)) + b) * 64 + h * WW + 16)
            wide[:, lines16, :] = full[:, b].astype(jnp.bfloat16)
            thin[:, lines16, :] = some[:, b]

    for t in range(frames):
        frame = lax.rem(shifts[0] + t, frames)
        sources = [jnp.maximum(frame - 2, 0), jnp.maximum(frame - 1, 0), frame]
        rest = thin[sources[0]]
        rest = rest + pltpu.roll(thin[sources[1]], CL, 1)
        rest = rest + pltpu.roll(thin[sources[2]], 2 * CL, 1)
        blocks = [wide[f] for f in sources] + [rest.astype(jnp.bfloat16)]
        for w in range(rows * cols // 64):
            a, b = divmod(w, cols // WW)
            window = (a * (frames // WT) + t // WT) * (cols // WW) + b
            start = window * CELLS + (t % WT) * 64
            for k in range(4):
                stacked[start : start + 64, k * LANES : (k + 1) * LANES] = blocks[k][w * 64 : w * 64 + 64]

    for copy in loads:
        copy.wait()
    for copy in later_loads:
        copy.start()

    total = frames * rows * cols
    for n in range(0, D, 256):
        weight = packed[:, :, :, n : n + 256].reshape(DEEP, 256)
        hidden = jnp.dot(stacked[...], weight, preferred_element_type=jnp.float32)
        conv[:, n : n + 256] = hidden
        grouped = hidden.reshape(total // 8, 8, 256)
        sums[:, n : n + 256] = jnp.sum(grouped, axis=0)
        squares[:, n : n + 256] = jnp.sum(grouped * grouped, axis=0)

    first_sums, second_sums = sums[...], squares[...]
    for by in (4, 2, 1):
        first_sums = first_sums + pltpu.roll(first_sums, by, 0)
        second_sums = second_sums + pltpu.roll(second_sums, by, 0)
    second_sums = second_sums + rows_of[0] * (2.0 * first_sums + total * rows_of[0])
    first_sums = first_sums + total * rows_of[0]

    sub = lax.broadcasted_iota(jnp.int32, (8, LANES), 0)
    lane8 = lax.broadcasted_iota(jnp.int32, (8, LANES), 1)
    width = D // GROUPS
    segments = []
    for i in range(SPAN // LANES):
        value = jnp.zeros((8, LANES), jnp.float32)
        for s in range(D // SPAN):
            lanes = slice(s * SPAN + i * LANES, s * SPAN + (i + 1) * LANES)
            value = jnp.where(sub == s, first_sums[:, lanes], value)
            value = jnp.where(sub == s + 4, second_sums[:, lanes], value)
        segments.append(value)
    table = jnp.zeros((8, LANES), jnp.float32)
    for j in range(SPAN // width):
        low, high = j * width, (j + 1) * width
        column = jnp.zeros((8, LANES), jnp.float32)
        for i in range(SPAN // LANES):
            start = i * LANES
            if low < start + LANES and high > start:
                inside = (lane8 >= low - start) & (lane8 < high - start)
                column = column + jnp.where(inside, segments[i], 0.0)
        table = jnp.where(lane8 == j, jnp.sum(column, axis=1, keepdims=True), table)

    one_row = jnp.zeros((8, LANES), jnp.float32)
    for k in range(8):
        here = (sub == k) & (lane8 // 8 == k)
        one_row = jnp.where(here, pltpu.roll(table, 8 * k, 1), one_row)
    for by in (4, 2, 1):
        one_row = one_row + pltpu.roll(one_row, by, 0)
    part[0] = one_row[:1]
    sent = []
    slot = 0
    for phase, group in enumerate(groups):
        for k, peer in enumerate(group):
            copy = pltpu.make_async_remote_copy(
                src_ref=part.at[phase],
                dst_ref=arrived.at[slot + k],
                send_sem=sum_send.at[phase],
                recv_sem=sum_recv.at[phase],
                device_id=peer,
                device_id_type=MESH,
            )
            copy.start()
        landed = arrived.at[pl.ds(slot, len(group))]
        whole = pltpu.make_async_copy(landed, landed, sum_recv.at[phase])
        whole.wait()
        sent.append(pltpu.make_async_copy(landed, landed, sum_send.at[phase]))
        part[phase + 1] = part[phase] + jnp.sum(arrived[slot : slot + len(group)], axis=0)
        slot += len(group)
    one_row = jnp.broadcast_to(part[len(groups)], (8, LANES))
    table = jnp.zeros((8, LANES), jnp.float32)
    for k in range(8):
        table = jnp.where(sub == k, pltpu.roll(one_row, (LANES - 8 * k) % LANES, 1), table)

    count = total * n_row * n_col * width
    mean = table * (1.0 / count)
    var = pltpu.roll(mean, 4, 0) - mean * mean
    scale = lax.rsqrt(var + EPS)
    for i in range(SPAN // LANES):
        mean_here = jnp.zeros((8, LANES), jnp.float32)
        scale_here = jnp.zeros((8, LANES), jnp.float32)
        for j in range(SPAN // width):
            low, high = j * width - i * LANES, (j + 1) * width - i * LANES
            if low < LANES and high > 0:
                inside = (lane8 >= low) & (lane8 < high)
                mean_here = jnp.where(inside, mean[:, j : j + 1], mean_here)
                scale_here = jnp.where(inside, scale[:, j : j + 1], scale_here)
        for s in range(D // SPAN):
            lanes = slice(s * SPAN + i * LANES, s * SPAN + (i + 1) * LANES)
            means[:, lanes] = mean_here[s : s + 1]
            scales[:, lanes] = scale_here[s : s + 1]
    steep = 0.5 * scales[...] * rows_of[1]
    slope[...] = steep
    offset[...] = (rows_of[0] - means[...]) * steep + 0.5 * rows_of[2]
    for copy in sent:
        copy.wait()
    for copy in halos:
        copy.wait_send()


STEPS = HEADS // 2


def attend_kernel(
    dims,
    way,
    latent,
    conv_weight,
    bias,
    gain,
    beta,
    shifts,
    qkv_weight,
    own_out,
    row_out,
    col_out,
    corner_out,
    feat,
    qkv,
    weights,
    own,
    edge,
    weight_sems,
    own_sems,
    row_send,
    row_recv,
    col_send,
    col_recv,
    corner_send,
    corner_recv,
    conv,
    slope,
    offset,
    *rest,
):
    frames, rows, cols = dims
    total = frames * rows * cols
    step = pl.program_id(0)
    n_row, n_col = lax.axis_size("row"), lax.axis_size("col")
    me_row, me_col = lax.axis_index("row"), lax.axis_index("col")
    to_row = {"row": lax.rem(me_row + (n_row - 1 if way else 1), n_row)}
    from_row = {"row": lax.rem(me_row + (1 if way else n_row - 1), n_row)}
    sides = [{"col": lax.rem(me_col + k, n_col)} for k in (1, n_col - 1)]
    across, deep = cols // WW, frames // WT
    row_edge = 0 if way else rows // WH - 1
    order = [row_edge] + [a for a in range(rows // WH) if a != row_edge]

    def sends(p, a):
        copies = []
        for side, peer in enumerate(sides):
            copies.append(
                pltpu.make_async_remote_copy(
                    src_ref=edge.at[side, p, a],
                    dst_ref=col_out.at[side, p, a],
                    send_sem=col_send,
                    recv_sem=col_recv,
                    device_id=peer,
                    device_id_type=MESH,
                )
            )
        if a == row_edge:
            lines = pl.ds(0 if way else 32, 32)
            copies.append(
                pltpu.make_async_remote_copy(
                    src_ref=own.at[p, pl.ds(a * across, across), :, lines],
                    dst_ref=row_out.at[p],
                    send_sem=row_send,
                    recv_sem=row_recv,
                    device_id=to_row,
                    device_id_type=MESH,
                )
            )
            lines = pl.ds(0 if way else 16, 16)
            for side, peer in enumerate(sides):
                copies.append(
                    pltpu.make_async_remote_copy(
                        src_ref=edge.at[side, p, a, :, lines],
                        dst_ref=corner_out.at[side, p],
                        send_sem=corner_send,
                        recv_sem=corner_recv,
                        device_id=to_row | peer,
                        device_id_type=MESH,
                    )
                )
        return copies

    def keep(p, a):
        rows_of = pl.ds(a * across, across)
        return pltpu.make_async_copy(own.at[p, rows_of], own_out.at[p, rows_of], own_sems)

    def loads(p):
        copies = []
        for j in range(3):
            columns = pl.ds(pl.multiple_of((j * STEPS + p) * PAIR, PAIR), PAIR)
            copies.append(
                pltpu.make_async_copy(
                    qkv_weight.at[:, columns], weights.at[p, j], weight_sems.at[p, j]
                )
            )
        return copies

    part = total // len(order)

    def lines_of(a):
        return slice(a * part, (a + 1) * part)

    def project(p, j, lines=slice(0, total)):
        slot = lax.rem(p, 2)
        qkv[slot, lines, j * PAIR : (j + 1) * PAIR] = jnp.dot(
            feat[lines, :], weights[p, j], preferred_element_type=jnp.float32
        ).astype(jnp.bfloat16)

    def features(lines, places):
        for k in places:
            n = slice(k * PAIR, (k + 1) * PAIR)
            half = conv[lines, n] * slope[:, n] + offset[:, n]
            feat[lines, n] = (half + half * jnp.tanh(half)).astype(jnp.bfloat16)

    sub = lax.broadcasted_iota(jnp.int32, (WH // 2, WW, HD), 1)

    def attention(p):
        source = lax.rem(p, 2)

        def part(item, j):
            window, head = item
            first = j * PAIR + head * HD
            return qkv[source, window * CELLS : (window + 1) * CELLS, first : first + HD]

        def score(item):
            return lax.dot_general(
                part(item, 0), part(item, 1), (((1,), (1,)), ((), ())), preferred_element_type=jnp.float32
            )

        def softmax(scores):
            most = [jnp.max(x, axis=-1, keepdims=True) for x in scores]
            powers = [
                jnp.exp2((x - m) * (math.log2(math.e) / HD**0.5)) for x, m in zip(scores, most)
            ]
            sums = [jnp.sum(x, axis=-1, keepdims=True) for x in powers]
            return [(x * (1.0 / t)).astype(jnp.bfloat16) for x, t in zip(powers, sums)]

        def items(a):
            return [(w, head) for head in range(2) for w in range(a * deep * across, (a + 1) * deep * across)]

        def store(a, item, result):
            window, head = item
            t2, b = divmod(window - a * deep * across, across)
            lanes = slice(head * HD, (head + 1) * HD)
            halves = result.reshape(WT, WH * WW, HD)
            for t in range(WT):
                own[p, a * across + b, t2 * WT + t, :, lanes] = halves[t].astype(jnp.bfloat16)
            lines = result.reshape(WT, WH // 2, 2, WW, HD)
            for side in range(2):
                if b != (0 if side else across - 1):
                    continue
                for t in range(WT):
                    even, odd = lines[t, :, 0], lines[t, :, 1]
                    if side:
                        packed = jnp.where(sub < 4, even, pltpu.roll(odd, 4, 1))
                    else:
                        packed = jnp.where(sub < 4, pltpu.roll(even, 4, 1), odd)
                    edge[side, p, a, t2 * WT + t, :, lanes] = packed.reshape(WH * HALF, HD).astype(
                        jnp.bfloat16
                    )

        def apply(names, probs):
            return [
                jnp.dot(x, part(item, 2), preferred_element_type=jnp.float32)
                for item, x in zip(names, probs)
            ]

        return items, score, softmax, apply, store

    def send(p, a):
        for copy in sends(p, a):
            copy.start()
        keep(p, a).start()

    def run(p, jobs):
        items, score, softmax, apply, store = attention(p)
        waiting = [score(item) for item in items(order[0])]
        for k, a in enumerate(order):
            jobs[k]()
            results = apply(items(a), softmax(waiting))
            if k + 1 < len(order):
                waiting = [score(item) for item in items(order[k + 1])]
            for item, result in zip(items(a), results):
                store(a, item, result)
        jobs[len(order)]()
        for a in order:
            send(p, a)

    last = STEPS - 1
    ahead, behind = lines_of(order[0]), lines_of(order[1])

    @pl.when(step == 0)
    def _():
        later_loads = [copy for p in range(STEPS) for copy in loads(p)]
        prepare(
            dims,
            later_loads,
            latent,
            conv_weight,
            bias,
            gain,
            beta,
            shifts,
            conv,
            slope,
            offset,
            *rest,
        )
        features(ahead, range(D // PAIR))
        for copy in loads(0):
            copy.wait()
        for j, places in enumerate((range(4), range(4, 7), range(7, D // PAIR))):
            features(behind, places)
            project(0, j, ahead)
        for j in range(3):
            project(0, j, behind)

    @pl.when((step > 0) & (step < last))
    def _():
        for copy in loads(step):
            copy.wait()
        run(step - 1, [functools.partial(project, step, j) for j in range(3)])

    @pl.when(step == last)
    def _():
        for copy in loads(last):
            copy.wait()
        run(last - 1, [functools.partial(project, last, j, ahead) for j in range(3)])

    @pl.when(step == STEPS)
    def _():
        items, score, softmax, apply, store = attention(last)
        waiting = [score(item) for item in items(order[0])]
        project(last, 0, behind)
        results = apply(items(order[0]), softmax(waiting))
        for item, result in zip(items(order[0]), results):
            store(order[0], item, result)
        send(last, order[0])
        project(last, 1, behind)
        waiting = [score(item) for item in items(order[1])]
        project(last, 2, behind)
        results = apply(items(order[1]), softmax(waiting))
        for item, result in zip(items(order[1]), results):
            store(order[1], item, result)
        send(last, order[1])

        for array, sems in (
            (own_out, (own_sems,)),
            (col_out, (col_send, col_recv)),
            (row_out, (row_send, row_recv)),
            (corner_out, (corner_send, corner_recv)),
        ):
            for sem in sems:
                pltpu.make_async_copy(array, array, sem).wait()


def attend(dims, way, latent, conv_weight, conv_bias, norm_gain, norm_bias, shifts, qkv_weight):
    frames, rows, cols = dims
    total = frames * rows * cols
    quarters = (rows // WH) * (cols // WW)
    n_row, n_col = lax.axis_size("row"), lax.axis_size("col")
    count = n_row * n_col - 1 if n_row * n_col <= ONE_PHASE else n_row + n_col - 2
    hbm = pl.BlockSpec(memory_space=pl.ANY)
    smem = pl.BlockSpec(memory_space=pltpu.SMEM)
    tile = pl.BlockSpec(latent.shape, lambda h: (0,) * latent.ndim, pipeline_mode=pl.Buffered(1))
    own = (STEPS, quarters, frames, WH * WW, PAIR)
    row = (STEPS, cols // WW, frames, HALF * WW, PAIR)
    col = (2, STEPS, rows // WH, frames, HALF * WH, PAIR)
    corner = (2, STEPS, frames, HALF * HALF, PAIR)
    dma = pltpu.SemaphoreType.DMA

    def narrow(*shape):
        return pltpu.VMEM(shape, jnp.bfloat16)

    def float32(*shape):
        return pltpu.VMEM(shape, jnp.float32)

    return pl.pallas_call(
        functools.partial(attend_kernel, dims, way),
        grid=(STEPS + 1,),
        out_shape=[jax.ShapeDtypeStruct(shape, jnp.bfloat16) for shape in (own, row, col, corner)],
        in_specs=[tile, hbm, hbm, hbm, hbm, smem, hbm],
        out_specs=[hbm] * 4,
        scratch_shapes=[
            narrow(total, D),
            narrow(2, total, 3 * PAIR),
            narrow(STEPS, 3, D, PAIR),
            narrow(*own),
            narrow(*col),
            dma((STEPS, 3)),
            dma,
            dma,
            dma,
            dma,
            dma,
            dma,
            dma,
            float32(total, D),
            float32(1, D),
            float32(1, D),
            narrow(total, DEEP),
            float32(frames, 32, DEEP),
            narrow(2, frames // 2, 16, 2 * LANES),
            narrow(2, frames, 16, LANES),
            narrow(2, frames // 2, 16, 2 * LANES),
            narrow(2, frames, 16, LANES),
            narrow(4, frames // 2, 16, LANES),
            float32(frames, 32, 3 * LANES),
            narrow(frames, rows * cols, LANES),
            float32(frames, rows * cols, LANES),
            narrow(4, 8, CL, D),
            float32(8, D),
            float32(8, D),
            float32(1, D),
            float32(1, D),
            float32(3, 1, D),
            float32(3, 1, LANES),
            float32(count, 1, LANES),
            dma((4,)),
            dma((8,)),
            dma((8,)),
            dma((2,)),
            dma((2,)),
            dma((3,)),
        ],
        compiler_params=pltpu.CompilerParams(
            collective_id=1 + way, has_side_effects=True, vmem_limit_bytes=60 * 1024 * 1024
        ),
    )(latent, conv_weight, conv_bias, norm_gain, norm_bias, shifts, qkv_weight)


def place_kernel(
    dims, shifts, own_in, row_in, col_in, corner_in, result, own, row, col, corner, out, field, in_sems, out_sems
):
    frames, rows, cols = dims
    across = cols // WW
    move_row = signed_shift(shifts[1], WH)
    move_col = signed_shift(shifts[2], WW)
    high, blocks = rows + HALF, cols // WW + 1
    turn = lax.rem(move_col + blocks * WW, blocks * WW)
    jump, slide = turn // WW, lax.rem(turn, WW)
    later = lax.broadcasted_iota(jnp.int32, (WW, PAIR), 0) >= slide

    def spread(value):
        lines = value.astype(jnp.float32).reshape(-1, 8, PAIR)
        low = lax.broadcasted_iota(jnp.int32, lines.shape, 1) < HALF
        other = pltpu.roll(lines, HALF, 1)
        pair = jnp.stack([jnp.where(low, lines, other), jnp.where(low, other, lines)], 1)
        return pair.reshape(-1, 8, PAIR)

    side = jnp.where(shifts[2] > HALF, 1, 0)

    def loads(t):
        pairs = ((own_in, own), (row_in, row), (col_in.at[side], col))
        copies = [
            pltpu.make_async_copy(x.at[:, :, t], y.at[:, :, t], in_sems.at[t, k])
            for k, (x, y) in enumerate(pairs)
        ]
        copies.append(pltpu.make_async_copy(corner_in.at[side, :, t], corner.at[:, t], in_sems.at[t, 3]))
        return copies

    def leave(t):
        frame = lax.rem(shifts[0] + t, frames)
        return pltpu.make_async_copy(out.at[t], result.at[frame], out_sems.at[t])

    for t in range(frames):
        for copy in loads(t):
            copy.start()

    @pl.loop(0, frames)
    def _(t):
        for copy in loads(t):
            copy.wait()
        for p in range(STEPS):
            for a in range(rows // WH):
                for b in range(across):
                    value = own[p, a * across + b, t].astype(jnp.float32)
                    field[p, a * WH : (a + 1) * WH, b] = value.reshape(WH, WW, PAIR)
                field[p, a * WH : (a + 1) * WH, across] = spread(col[p, a, t])
            for b in range(across):
                value = row[p, b, t].astype(jnp.float32)
                field[p, rows:, b] = value.reshape(HALF, WW, PAIR)
            field[p, rows:, across] = spread(corner[p, t])
            lanes = slice(p * PAIR, (p + 1) * PAIR)
            for y in range(rows):
                line = lax.rem(y - move_row + high, high)
                turned = [
                    pltpu.roll(field[p, line, lax.rem(k - jump + 2 * blocks, blocks)], slide, 0)
                    for k in range(-1, across)
                ]
                pieces = [jnp.where(later, turned[k + 1], turned[k]) for k in range(across)]
                out[t, y, :, lanes] = jnp.concatenate(pieces, 0).astype(jnp.bfloat16)
        leave(t).start()

    for t in range(frames):
        leave(t).wait()


def place(dims, shifts, own, row, col, corner):
    frames, rows, cols = dims
    hbm = pl.BlockSpec(memory_space=pl.ANY)
    shape = (frames, rows, cols, HEADS * HD)
    shapes = (own.shape, row.shape, col.shape[1:], corner.shape[1:])
    scratch = [pltpu.VMEM(x, jnp.bfloat16) for x in shapes]
    return pl.pallas_call(
        functools.partial(place_kernel, dims),
        in_specs=[pl.BlockSpec(memory_space=pltpu.SMEM)] + [hbm] * 4,
        out_specs=hbm,
        out_shape=jax.ShapeDtypeStruct(shape, jnp.bfloat16),
        scratch_shapes=scratch
        + [
            pltpu.VMEM(shape, jnp.bfloat16),
            pltpu.VMEM((STEPS, rows + HALF, cols // WW + 1, WW, PAIR), jnp.float32),
            pltpu.SemaphoreType.DMA((frames, 4)),
            pltpu.SemaphoreType.DMA((frames,)),
        ],
        compiler_params=pltpu.CompilerParams(vmem_limit_bytes=60 * 1024 * 1024),
    )(shifts, own, row, col, corner)


def per_device(latent, conv_weight, conv_bias, norm_gain, norm_bias, qkv_weight, shifts):
    dims = (latent.shape[0], latent.shape[1], latent.shape[2])
    branches = [functools.partial(attend, dims, way) for way in range(2)]
    results = lax.cond(
        shifts[1] > HALF,
        branches[1],
        branches[0],
        latent,
        conv_weight.reshape(3, 3, 3, CL, D),
        conv_bias,
        norm_gain,
        norm_bias,
        shifts,
        qkv_weight,
    )
    return place(dims, shifts, *results)


def solution(mesh):
    in_specs = (P(None, "row", "col", None), P(), P(), P(), P(), P(), P())
    out_specs = P(None, "row", "col", None)
    return jax.shard_map(
        per_device, mesh=mesh, in_specs=in_specs, out_specs=out_specs, check_vma=False
    )
```

```python
import functools
import math

import jax
import jax.numpy as jnp
from jax import lax
from jax.experimental import pallas as pl
from jax.experimental.pallas import tpu as pltpu
from jax.sharding import PartitionSpec as P

CL = 16
GROUPS = 32
D = 2560
HEADS = 10
HD = 128
WT = 2
WH = 8
WW = 8
HALF = 4


def signed_shift(shift, window):
    return jnp.where(shift <= HALF, shift, shift - window)


CELLS = WT * WH * WW
PAIR = 2 * HD


MESH = pl.DeviceIdType.MESH
LANES = 128
TAPS = 9
DEEP = 4 * LANES
SPAN = 640
EPS = 1e-05
ONE_PHASE = 32


def prepare(
    dims,
    later_loads,
    latent,
    conv_weight,
    bias,
    gain,
    beta,
    shifts,
    conv,
    slope,
    offset,
    stacked,
    field,
    rim_cols,
    rim_rows,
    from_cols,
    from_rows,
    from_corners,
    moved,
    wide,
    thin,
    packed,
    sums,
    squares,
    means,
    scales,
    rows_of,
    part,
    arrived,
    weight_sems,
    halo_send,
    halo_recv,
    sum_send,
    sum_recv,
    row_sems,
):
    frames, rows, cols = dims
    n_row, n_col = lax.axis_size("row"), lax.axis_size("col")
    me_row, me_col = lax.axis_index("row"), lax.axis_index("col")
    down, up = lax.rem(me_row + 1, n_row), lax.rem(me_row + n_row - 1, n_row)
    right, left = lax.rem(me_col + 1, n_col), lax.rem(me_col + n_col - 1, n_col)

    by_row = [lax.rem(me_row + k, n_row) for k in range(n_row)]
    by_col = [lax.rem(me_col + k, n_col) for k in range(n_col)]
    corners = [{"row": r, "col": c} for r in (down, up) for c in (right, left)]
    if n_row * n_col <= ONE_PHASE:
        groups = [[{"row": r, "col": c} for r in by_row for c in by_col][1:]]
        peers = groups[0]
    else:
        groups = [[{"col": c} for c in by_col[1:]], [{"row": r} for r in by_row[1:]]]
        peers = groups[0] + groups[1] + corners
    barrier = pltpu.get_barrier_semaphore()
    for peer in peers:
        pl.semaphore_signal(barrier, inc=1, device_id=peer, device_id_type=MESH)

    lines = []
    for k, value in enumerate((bias, gain, beta)):
        lines.append(pltpu.make_async_copy(value, rows_of.at[k, 0], row_sems.at[k]))
        lines[-1].start()
    lane16 = lax.broadcasted_iota(jnp.int32, (CL, LANES), 1)
    chan = lax.broadcasted_iota(jnp.int32, (CL, LANES), 0)
    for half in range(2):
        total = jnp.zeros((frames * cols, LANES), jnp.float32)
        for y in range(8):
            pick = jnp.where(lane16 == chan + y * CL, 1.0, 0.0).astype(jnp.bfloat16)
            line = latent[:, half * 8 + y].reshape(frames * cols, CL)
            total = total + jnp.dot(line, pick, preferred_element_type=jnp.float32)
        lanes = slice((1 + half) * LANES, (2 + half) * LANES)
        field[:, 8:24, lanes] = total.reshape(frames, cols, LANES)

    rim_cols[0] = field[:, 16:24, LANES : 3 * LANES].reshape(frames // 2, 16, 2 * LANES).astype(jnp.bfloat16)
    rim_cols[1] = field[:, 8:16, LANES : 3 * LANES].reshape(frames // 2, 16, 2 * LANES).astype(jnp.bfloat16)
    rim_rows[0] = field[:, 8:24, 2 * LANES : 3 * LANES].astype(jnp.bfloat16)
    rim_rows[1] = field[:, 8:24, LANES : 2 * LANES].astype(jnp.bfloat16)

    pl.semaphore_wait(barrier, len(peers))

    low, high = pl.ds(0, LANES), pl.ds(LANES, LANES)
    plan = [
        ({"col": right}, rim_cols.at[0], from_cols.at[0]),
        ({"col": left}, rim_cols.at[1], from_cols.at[1]),
        ({"row": down}, rim_rows.at[0], from_rows.at[0]),
        ({"row": up}, rim_rows.at[1], from_rows.at[1]),
        (corners[0], rim_cols.at[0, :, :, high], from_corners.at[0]),
        (corners[1], rim_cols.at[1, :, :, high], from_corners.at[1]),
        (corners[2], rim_cols.at[0, :, :, low], from_corners.at[2]),
        (corners[3], rim_cols.at[1, :, :, low], from_corners.at[3]),
    ]
    halos = []
    for k, (peer, source, target) in enumerate(plan):
        halos.append(
            pltpu.make_async_remote_copy(
                src_ref=source,
                dst_ref=target,
                send_sem=halo_send.at[k],
                recv_sem=halo_recv.at[k],
                device_id=peer,
                device_id_type=MESH,
            )
        )
        halos[-1].start()

    blocks = pl.ds(0, 3)
    loads = [
        pltpu.make_async_copy(conv_weight.at[:, :, 0], packed.at[blocks, pl.ds(0, 3)], weight_sems.at[0]),
        pltpu.make_async_copy(conv_weight.at[:, :, 1], packed.at[blocks, pl.ds(3, 3)], weight_sems.at[1]),
        pltpu.make_async_copy(
            conv_weight.at[:, pl.ds(0, 2), 2], packed.at[blocks, pl.ds(6, 2)], weight_sems.at[2]
        ),
        pltpu.make_async_copy(conv_weight.at[:, 2, 2], packed.at[3, pl.ds(0, 3)], weight_sems.at[3]),
    ]
    for copy in loads:
        copy.start()
    packed[3, 3:] = jnp.zeros((5, CL, D), jnp.bfloat16)

    move_row = signed_shift(shifts[1], WH)
    move_col = signed_shift(shifts[2], WW)
    for copy in lines:
        copy.wait()
    for copy in halos:
        copy.wait_recv()
    wide_lanes = slice(LANES, 3 * LANES)
    for k, at in enumerate((slice(0, 8), slice(24, 32))):
        field[:, at, wide_lanes] = from_cols[k].astype(jnp.float32).reshape(frames, 8, 2 * LANES)
    for k, lanes in enumerate((slice(0, LANES), slice(3 * LANES, DEEP))):
        field[:, 8:24, lanes] = from_rows[k].astype(jnp.float32)
        for side, at in enumerate((slice(0, 8), slice(24, 32))):
            value = from_corners[2 * k + side].astype(jnp.float32)
            field[:, at, lanes] = value.reshape(frames, 8, LANES)

    turned = pltpu.roll(field[...].reshape(frames * 32, DEEP), 400 - 16 * move_row, 1)
    turned = turned[:, : 3 * LANES].reshape(frames, 32, 3 * LANES)
    moved[...] = pltpu.roll(turned, 25 - move_col, 1)

    lane = lax.broadcasted_iota(jnp.int32, (frames * cols, LANES), 1)
    place = lax.broadcasted_iota(jnp.int32, (frames * cols, LANES), 0) % cols
    wide_cols, wide_rows = n_col * cols, n_row * rows
    at_col = lax.rem(me_col * cols + move_col + place + wide_cols, wide_cols)
    pieces = []
    for c in range(3):
        piece = moved[:, c : c + cols, :].reshape(frames * cols, 3 * LANES)
        parts = [piece[:, k * LANES : (k + 1) * LANES] for k in range(3)]
        if c == 0:
            parts = [jnp.where(at_col == 0, 0.0, p) for p in parts]
        if c == 2:
            parts = [jnp.where(at_col == wide_cols - 1, 0.0, p) for p in parts]
        pieces.append(parts)
    row_tap = (lane // CL) % 3

    def line_of(y):
        at_row = lax.rem(me_row * rows + move_row + y + wide_rows, wide_rows)
        turned = []
        for c in range(3):
            k, start = divmod(y * CL, LANES)
            value = pieces[c][k]
            if start + 48 > LANES:
                value = jnp.where(lane < start + 48 - LANES, pieces[c][k + 1], value)
            turned.append(pltpu.roll(value, (c * 48 - start) % LANES, 1))
        full = jnp.where(lane < 48, turned[0], jnp.where(lane < 96, turned[1], turned[2]))
        gone = jnp.where(at_row == 0, 0, -1)
        full = jnp.where(row_tap == gone, 0.0, full)
        gone = jnp.where(at_row == wide_rows - 1, 2, -1)
        full = jnp.where(row_tap == gone, 0.0, full)
        some = jnp.where(lane < jnp.where(at_row == wide_rows - 1, 0, CL), turned[2], 0.0)
        return full, some

    for y in range(0, rows, 2):
        fulls, somes = zip(*[line_of(y + k) for k in range(2)])
        a, h = divmod(y, WH)
        full = jnp.concatenate([v.reshape(frames, cols // WW, WW, LANES) for v in fulls], 2)
        some = jnp.concatenate([v.reshape(frames, cols // WW, WW, LANES) for v in somes], 2)
        for b in range(cols // WW):
            lines16 = slice(((a * (cols // WW)) + b) * 64 + h * WW, ((a * (cols // WW)) + b) * 64 + h * WW + 16)
            wide[:, lines16, :] = full[:, b].astype(jnp.bfloat16)
            thin[:, lines16, :] = some[:, b]

    for t in range(frames):
        frame = lax.rem(shifts[0] + t, frames)
        sources = [jnp.maximum(frame - 2, 0), jnp.maximum(frame - 1, 0), frame]
        rest = thin[sources[0]]
        rest = rest + pltpu.roll(thin[sources[1]], CL, 1)
        rest = rest + pltpu.roll(thin[sources[2]], 2 * CL, 1)
        blocks = [wide[f] for f in sources] + [rest.astype(jnp.bfloat16)]
        for w in range(rows * cols // 64):
            a, b = divmod(w, cols // WW)
            window = (a * (frames // WT) + t // WT) * (cols // WW) + b
            start = window * CELLS + (t % WT) * 64
            for k in range(4):
                stacked[start : start + 64, k * LANES : (k + 1) * LANES] = blocks[k][w * 64 : w * 64 + 64]

    for copy in loads:
        copy.wait()
    for copy in later_loads:
        copy.start()

    total = frames * rows * cols

    @pl.loop(0, 2)
    def _(half):
        for k in range(D // 512):
            n = pl.ds(pl.multiple_of(half * (D // 2) + k * 256, 256), 256)
            weight = packed[:, :, :, n].reshape(DEEP, 256)
            hidden = jnp.dot(stacked[...], weight, preferred_element_type=jnp.float32)
            conv[:, n] = hidden
            grouped = hidden.reshape(total // 8, 8, 256)
            sums[:, n] = jnp.sum(grouped, axis=0)
            squares[:, n] = jnp.sum(grouped * grouped, axis=0)

    first_sums, second_sums = sums[...], squares[...]
    for by in (4, 2, 1):
        first_sums = first_sums + pltpu.roll(first_sums, by, 0)
        second_sums = second_sums + pltpu.roll(second_sums, by, 0)
    second_sums = second_sums + rows_of[0] * (2.0 * first_sums + total * rows_of[0])
    first_sums = first_sums + total * rows_of[0]

    sub = lax.broadcasted_iota(jnp.int32, (8, LANES), 0)
    lane8 = lax.broadcasted_iota(jnp.int32, (8, LANES), 1)
    width = D // GROUPS
    segments = []
    for i in range(SPAN // LANES):
        value = jnp.zeros((8, LANES), jnp.float32)
        for s in range(D // SPAN):
            lanes = slice(s * SPAN + i * LANES, s * SPAN + (i + 1) * LANES)
            value = jnp.where(sub == s, first_sums[:, lanes], value)
            value = jnp.where(sub == s + 4, second_sums[:, lanes], value)
        segments.append(value)
    table = jnp.zeros((8, LANES), jnp.float32)
    for j in range(SPAN // width):
        low, high = j * width, (j + 1) * width
        column = jnp.zeros((8, LANES), jnp.float32)
        for i in range(SPAN // LANES):
            start = i * LANES
            if low < start + LANES and high > start:
                inside = (lane8 >= low - start) & (lane8 < high - start)
                column = column + jnp.where(inside, segments[i], 0.0)
        table = jnp.where(lane8 == j, jnp.sum(column, axis=1, keepdims=True), table)

    one_row = jnp.zeros((8, LANES), jnp.float32)
    for k in range(8):
        here = (sub == k) & (lane8 // 8 == k)
        one_row = jnp.where(here, pltpu.roll(table, 8 * k, 1), one_row)
    for by in (4, 2, 1):
        one_row = one_row + pltpu.roll(one_row, by, 0)
    part[0] = one_row[:1]
    sent = []
    slot = 0
    for phase, group in enumerate(groups):
        for k, peer in enumerate(group):
            copy = pltpu.make_async_remote_copy(
                src_ref=part.at[phase],
                dst_ref=arrived.at[slot + k],
                send_sem=sum_send.at[phase],
                recv_sem=sum_recv.at[phase],
                device_id=peer,
                device_id_type=MESH,
            )
            copy.start()
        landed = arrived.at[pl.ds(slot, len(group))]
        whole = pltpu.make_async_copy(landed, landed, sum_recv.at[phase])
        whole.wait()
        sent.append(pltpu.make_async_copy(landed, landed, sum_send.at[phase]))
        part[phase + 1] = part[phase] + jnp.sum(arrived[slot : slot + len(group)], axis=0)
        slot += len(group)
    one_row = jnp.broadcast_to(part[len(groups)], (8, LANES))
    table = jnp.zeros((8, LANES), jnp.float32)
    for k in range(8):
        table = jnp.where(sub == k, pltpu.roll(one_row, (LANES - 8 * k) % LANES, 1), table)

    count = total * n_row * n_col * width
    mean = table * (1.0 / count)
    var = pltpu.roll(mean, 4, 0) - mean * mean
    scale = lax.rsqrt(var + EPS)
    for i in range(SPAN // LANES):
        mean_here = jnp.zeros((8, LANES), jnp.float32)
        scale_here = jnp.zeros((8, LANES), jnp.float32)
        for j in range(SPAN // width):
            low, high = j * width - i * LANES, (j + 1) * width - i * LANES
            if low < LANES and high > 0:
                inside = (lane8 >= low) & (lane8 < high)
                mean_here = jnp.where(inside, mean[:, j : j + 1], mean_here)
                scale_here = jnp.where(inside, scale[:, j : j + 1], scale_here)
        for s in range(D // SPAN):
            lanes = slice(s * SPAN + i * LANES, s * SPAN + (i + 1) * LANES)
            means[:, lanes] = mean_here[s : s + 1]
            scales[:, lanes] = scale_here[s : s + 1]
    steep = 0.5 * scales[...] * rows_of[1]
    slope[...] = steep
    offset[...] = (rows_of[0] - means[...]) * steep + 0.5 * rows_of[2]
    for copy in sent:
        copy.wait()
    for copy in halos:
        copy.wait_send()


STEPS = HEADS // 2


def columns_of(k):
    if isinstance(k, int):
        return slice(k * PAIR, (k + 1) * PAIR)
    return pl.ds(pl.multiple_of(k * PAIR, PAIR), PAIR)


def attend_kernel(
    dims,
    way,
    latent,
    conv_weight,
    bias,
    gain,
    beta,
    shifts,
    qkv_weight,
    own_out,
    row_out,
    col_out,
    corner_out,
    feat,
    qkv,
    weights,
    own,
    edge,
    weight_sems,
    own_sems,
    row_send,
    row_recv,
    col_send,
    col_recv,
    corner_send,
    corner_recv,
    conv,
    slope,
    offset,
    *rest,
):
    frames, rows, cols = dims
    total = frames * rows * cols
    step = pl.program_id(0)
    n_row, n_col = lax.axis_size("row"), lax.axis_size("col")
    me_row, me_col = lax.axis_index("row"), lax.axis_index("col")
    to_row = {"row": lax.rem(me_row + (n_row - 1 if way else 1), n_row)}
    from_row = {"row": lax.rem(me_row + (1 if way else n_row - 1), n_row)}
    sides = [{"col": lax.rem(me_col + k, n_col)} for k in (1, n_col - 1)]
    across, deep = cols // WW, frames // WT
    row_edge = 0 if way else rows // WH - 1
    order = [row_edge] + [a for a in range(rows // WH) if a != row_edge]

    def sends(p, a):
        copies = []
        for side, peer in enumerate(sides):
            copies.append(
                pltpu.make_async_remote_copy(
                    src_ref=edge.at[side, p, a],
                    dst_ref=col_out.at[side, p, a],
                    send_sem=col_send,
                    recv_sem=col_recv,
                    device_id=peer,
                    device_id_type=MESH,
                )
            )
        if a == row_edge:
            lines = pl.ds(0 if way else 32, 32)
            copies.append(
                pltpu.make_async_remote_copy(
                    src_ref=own.at[p, pl.ds(a * across, across), :, lines],
                    dst_ref=row_out.at[p],
                    send_sem=row_send,
                    recv_sem=row_recv,
                    device_id=to_row,
                    device_id_type=MESH,
                )
            )
            lines = pl.ds(0 if way else 16, 16)
            for side, peer in enumerate(sides):
                copies.append(
                    pltpu.make_async_remote_copy(
                        src_ref=edge.at[side, p, a, :, lines],
                        dst_ref=corner_out.at[side, p],
                        send_sem=corner_send,
                        recv_sem=corner_recv,
                        device_id=to_row | peer,
                        device_id_type=MESH,
                    )
                )
        return copies

    def keep(p, a):
        rows_of = pl.ds(a * across, across)
        return pltpu.make_async_copy(own.at[p, rows_of], own_out.at[p, rows_of], own_sems)

    def loads(p):
        copies = []
        for j in range(3):
            columns = pl.ds(pl.multiple_of((j * STEPS + p) * PAIR, PAIR), PAIR)
            copies.append(
                pltpu.make_async_copy(
                    qkv_weight.at[:, columns], weights.at[p, j], weight_sems.at[p, j]
                )
            )
        return copies

    part = total // len(order)

    def lines_of(a):
        return slice(a * part, (a + 1) * part)

    def project(p, j, lines=slice(0, total)):
        slot = lax.rem(p, 2)
        qkv[slot, lines, columns_of(j)] = jnp.dot(
            feat[lines, :], weights[p, j], preferred_element_type=jnp.float32
        ).astype(jnp.bfloat16)

    def features(lines, places):
        for k in places:
            n = columns_of(k)
            half = conv[lines, n] * slope[:, n] + offset[:, n]
            feat[lines, n] = (half + half * jnp.tanh(half)).astype(jnp.bfloat16)

    sub = lax.broadcasted_iota(jnp.int32, (WH // 2, WW, HD), 1)

    def attention(p):
        source = lax.rem(p, 2)

        def part(item, j):
            window, head = item
            first = j * PAIR + head * HD
            return qkv[source, window * CELLS : (window + 1) * CELLS, first : first + HD]

        def score(item):
            return lax.dot_general(
                part(item, 0), part(item, 1), (((1,), (1,)), ((), ())), preferred_element_type=jnp.float32
            )

        def softmax(scores):
            most = [jnp.max(x, axis=-1, keepdims=True) for x in scores]
            powers = [
                jnp.exp2((x - m) * (math.log2(math.e) / HD**0.5)) for x, m in zip(scores, most)
            ]
            sums = [jnp.sum(x, axis=-1, keepdims=True) for x in powers]
            return [(x * (1.0 / t)).astype(jnp.bfloat16) for x, t in zip(powers, sums)]

        def items(a):
            return [(w, head) for head in range(2) for w in range(a * deep * across, (a + 1) * deep * across)]

        def store(a, item, result):
            window, head = item
            t2, b = divmod(window - a * deep * across, across)
            lanes = slice(head * HD, (head + 1) * HD)
            halves = result.reshape(WT, WH * WW, HD)
            for t in range(WT):
                own[p, a * across + b, t2 * WT + t, :, lanes] = halves[t].astype(jnp.bfloat16)
            lines = result.reshape(WT, WH // 2, 2, WW, HD)
            for side in range(2):
                if b != (0 if side else across - 1):
                    continue
                for t in range(WT):
                    even, odd = lines[t, :, 0], lines[t, :, 1]
                    if side:
                        packed = jnp.where(sub < 4, even, pltpu.roll(odd, 4, 1))
                    else:
                        packed = jnp.where(sub < 4, pltpu.roll(even, 4, 1), odd)
                    edge[side, p, a, t2 * WT + t, :, lanes] = packed.reshape(WH * HALF, HD).astype(
                        jnp.bfloat16
                    )

        def apply(names, probs):
            return [
                jnp.dot(x, part(item, 2), preferred_element_type=jnp.float32)
                for item, x in zip(names, probs)
            ]

        return items, score, softmax, apply, store

    def send(p, a):
        for copy in sends(p, a):
            copy.start()
        keep(p, a).start()

    def run(p, jobs):
        items, score, softmax, apply, store = attention(p)
        waiting = [score(item) for item in items(order[0])]
        for k, a in enumerate(order):
            jobs[k]()
            results = apply(items(a), softmax(waiting))
            if k + 1 < len(order):
                waiting = [score(item) for item in items(order[k + 1])]
            for item, result in zip(items(a), results):
                store(a, item, result)
        jobs[len(order)]()
        for a in order:
            send(p, a)

    last = STEPS - 1
    ahead, behind = lines_of(order[0]), lines_of(order[1])

    @pl.when(step == 0)
    def _():
        later_loads = [copy for p in range(STEPS) for copy in loads(p)]
        prepare(
            dims,
            later_loads,
            latent,
            conv_weight,
            bias,
            gain,
            beta,
            shifts,
            conv,
            slope,
            offset,
            *rest,
        )
        features(ahead, range(D // PAIR))
        for copy in loads(0):
            copy.wait()
        for j, places in enumerate((range(4), range(4, 7), range(7, D // PAIR))):
            features(behind, places)
            project(0, j, ahead)
        for j in range(3):
            project(0, j, behind)

    def finish(p, a, waiting, parts):
        items, score, softmax, apply, store = parts
        results = apply(items(a), softmax(waiting))
        for item, result in zip(items(a), results):
            store(a, item, result)

    @pl.when((step > 0) & (step < last - 1))
    def _():
        for copy in loads(step):
            copy.wait()
        run(step - 1, [functools.partial(project, step, j) for j in range(3)])

    @pl.when(step == last - 1)
    def _():
        for p in (last - 1, last):
            for copy in loads(p):
                copy.wait()
        run(last - 2, [functools.partial(project, last - 1, j, ahead) for j in range(3)])

    @pl.when((step == last) | (step == last + 1))
    def _():
        p, other = step - 1, 2 * last - step
        start = jnp.where(step == last, ahead.start, behind.start)
        lines = pl.ds(pl.multiple_of(start, part), part)
        parts = attention(p)
        waiting = [parts[1](item) for item in parts[0](order[0])]
        project(other, 0, lines)
        finish(p, order[0], waiting, parts)
        send(p, order[0])
        project(other, 1, lines)
        project(other, 2, lines)

    @pl.when(step == last + 2)
    def _():
        parts = attention(last - 1)
        waiting = [parts[1](item) for item in parts[0](order[1])]
        project(last, 0, behind)
        finish(last - 1, order[1], waiting, parts)
        send(last - 1, order[1])
        project(last, 1, behind)
        parts = attention(last)
        waiting = [parts[1](item) for item in parts[0](order[1])]
        project(last, 2, behind)
        finish(last, order[1], waiting, parts)
        send(last, order[1])

        for array, sems in (
            (own_out, (own_sems,)),
            (col_out, (col_send, col_recv)),
            (row_out, (row_send, row_recv)),
            (corner_out, (corner_send, corner_recv)),
        ):
            for sem in sems:
                pltpu.make_async_copy(array, array, sem).wait()


def attend(dims, way, latent, conv_weight, conv_bias, norm_gain, norm_bias, shifts, qkv_weight):
    frames, rows, cols = dims
    total = frames * rows * cols
    quarters = (rows // WH) * (cols // WW)
    n_row, n_col = lax.axis_size("row"), lax.axis_size("col")
    count = n_row * n_col - 1 if n_row * n_col <= ONE_PHASE else n_row + n_col - 2
    hbm = pl.BlockSpec(memory_space=pl.ANY)
    smem = pl.BlockSpec(memory_space=pltpu.SMEM)
    tile = pl.BlockSpec(latent.shape, lambda h: (0,) * latent.ndim, pipeline_mode=pl.Buffered(1))
    own = (STEPS, quarters, frames, WH * WW, PAIR)
    row = (STEPS, cols // WW, frames, HALF * WW, PAIR)
    col = (2, STEPS, rows // WH, frames, HALF * WH, PAIR)
    corner = (2, STEPS, frames, HALF * HALF, PAIR)
    dma = pltpu.SemaphoreType.DMA

    def narrow(*shape):
        return pltpu.VMEM(shape, jnp.bfloat16)

    def float32(*shape):
        return pltpu.VMEM(shape, jnp.float32)

    return pl.pallas_call(
        functools.partial(attend_kernel, dims, way),
        grid=(STEPS + 2,),
        out_shape=[jax.ShapeDtypeStruct(shape, jnp.bfloat16) for shape in (own, row, col, corner)],
        in_specs=[tile, hbm, hbm, hbm, hbm, smem, hbm],
        out_specs=[hbm] * 4,
        scratch_shapes=[
            narrow(total, D),
            narrow(2, total, 3 * PAIR),
            narrow(STEPS, 3, D, PAIR),
            narrow(*own),
            narrow(*col),
            dma((STEPS, 3)),
            dma,
            dma,
            dma,
            dma,
            dma,
            dma,
            dma,
            float32(total, D),
            float32(1, D),
            float32(1, D),
            narrow(total, DEEP),
            float32(frames, 32, DEEP),
            narrow(2, frames // 2, 16, 2 * LANES),
            narrow(2, frames, 16, LANES),
            narrow(2, frames // 2, 16, 2 * LANES),
            narrow(2, frames, 16, LANES),
            narrow(4, frames // 2, 16, LANES),
            float32(frames, 32, 3 * LANES),
            narrow(frames, rows * cols, LANES),
            float32(frames, rows * cols, LANES),
            narrow(4, 8, CL, D),
            float32(8, D),
            float32(8, D),
            float32(1, D),
            float32(1, D),
            float32(3, 1, D),
            float32(3, 1, LANES),
            float32(count, 1, LANES),
            dma((4,)),
            dma((8,)),
            dma((8,)),
            dma((2,)),
            dma((2,)),
            dma((3,)),
        ],
        compiler_params=pltpu.CompilerParams(
            collective_id=1 + way, has_side_effects=True, vmem_limit_bytes=60 * 1024 * 1024
        ),
    )(latent, conv_weight, conv_bias, norm_gain, norm_bias, shifts, qkv_weight)


def place_kernel(
    dims, shifts, own_in, row_in, col_in, corner_in, result, own, row, col, corner, out, field, in_sems, out_sems
):
    frames, rows, cols = dims
    across = cols // WW
    move_row = signed_shift(shifts[1], WH)
    move_col = signed_shift(shifts[2], WW)
    high, blocks = rows + HALF, cols // WW + 1
    turn = lax.rem(move_col + blocks * WW, blocks * WW)
    jump, slide = turn // WW, lax.rem(turn, WW)
    later = lax.broadcasted_iota(jnp.int32, (WW, PAIR), 0) >= slide

    def spread(value):
        lines = value.astype(jnp.float32).reshape(-1, 8, PAIR)
        low = lax.broadcasted_iota(jnp.int32, lines.shape, 1) < HALF
        other = pltpu.roll(lines, HALF, 1)
        pair = jnp.stack([jnp.where(low, lines, other), jnp.where(low, other, lines)], 1)
        return pair.reshape(-1, 8, PAIR)

    side = jnp.where(shifts[2] > HALF, 1, 0)

    def loads(t):
        pairs = ((own_in, own), (row_in, row), (col_in.at[side], col))
        copies = [
            pltpu.make_async_copy(x.at[:, :, t], y.at[:, :, t], in_sems.at[t, k])
            for k, (x, y) in enumerate(pairs)
        ]
        copies.append(pltpu.make_async_copy(corner_in.at[side, :, t], corner.at[:, t], in_sems.at[t, 3]))
        return copies

    def leave(t):
        frame = lax.rem(shifts[0] + t, frames)
        return pltpu.make_async_copy(out.at[t], result.at[frame], out_sems.at[t])

    for t in range(frames):
        for copy in loads(t):
            copy.start()

    @pl.loop(0, frames)
    def _(t):
        for copy in loads(t):
            copy.wait()
        for p in range(STEPS):
            for a in range(rows // WH):
                for b in range(across):
                    value = own[p, a * across + b, t].astype(jnp.float32)
                    field[p, a * WH : (a + 1) * WH, b] = value.reshape(WH, WW, PAIR)
                field[p, a * WH : (a + 1) * WH, across] = spread(col[p, a, t])
            for b in range(across):
                value = row[p, b, t].astype(jnp.float32)
                field[p, rows:, b] = value.reshape(HALF, WW, PAIR)
            field[p, rows:, across] = spread(corner[p, t])
            lanes = slice(p * PAIR, (p + 1) * PAIR)
            for y in range(rows):
                line = lax.rem(y - move_row + high, high)
                turned = [
                    pltpu.roll(field[p, line, lax.rem(k - jump + 2 * blocks, blocks)], slide, 0)
                    for k in range(-1, across)
                ]
                pieces = [jnp.where(later, turned[k + 1], turned[k]) for k in range(across)]
                out[t, y, :, lanes] = jnp.concatenate(pieces, 0).astype(jnp.bfloat16)
        leave(t).start()

    for t in range(frames):
        leave(t).wait()


def place(dims, shifts, own, row, col, corner):
    frames, rows, cols = dims
    hbm = pl.BlockSpec(memory_space=pl.ANY)
    shape = (frames, rows, cols, HEADS * HD)
    shapes = (own.shape, row.shape, col.shape[1:], corner.shape[1:])
    scratch = [pltpu.VMEM(x, jnp.bfloat16) for x in shapes]
    return pl.pallas_call(
        functools.partial(place_kernel, dims),
        in_specs=[pl.BlockSpec(memory_space=pltpu.SMEM)] + [hbm] * 4,
        out_specs=hbm,
        out_shape=jax.ShapeDtypeStruct(shape, jnp.bfloat16),
        scratch_shapes=scratch
        + [
            pltpu.VMEM(shape, jnp.bfloat16),
            pltpu.VMEM((STEPS, rows + HALF, cols // WW + 1, WW, PAIR), jnp.float32),
            pltpu.SemaphoreType.DMA((frames, 4)),
            pltpu.SemaphoreType.DMA((frames,)),
        ],
        compiler_params=pltpu.CompilerParams(vmem_limit_bytes=60 * 1024 * 1024),
    )(shifts, own, row, col, corner)


def per_device(latent, conv_weight, conv_bias, norm_gain, norm_bias, qkv_weight, shifts):
    dims = (latent.shape[0], latent.shape[1], latent.shape[2])
    branches = [functools.partial(attend, dims, way) for way in range(2)]
    results = lax.cond(
        shifts[1] > HALF,
        branches[1],
        branches[0],
        latent,
        conv_weight.reshape(3, 3, 3, CL, D),
        conv_bias,
        norm_gain,
        norm_bias,
        shifts,
        qkv_weight,
    )
    return place(dims, shifts, *results)


def solution(mesh):
    in_specs = (P(None, "row", "col", None), P(), P(), P(), P(), P(), P())
    out_specs = P(None, "row", "col", None)
    return jax.shard_map(
        per_device, mesh=mesh, in_specs=in_specs, out_specs=out_specs, check_vma=False
    )
```
